128 devices in a mesh: group: 4 (over x), col: 8 (over y_lo, z), row: 4 (over y_hi, core).
Axes of the slice: x: 4, y: 4 (y_hi: 2, y_lo: 2; y = y_hi * 2 + y_lo), z: 4, core: 2. Of those that a mesh axis runs over, the one named last changes fastest.
Arguments:
- latent: bfloat16 [256, 1024, 320], P('group', ('col', 'row')), may hold values from -6 to 6
- control: bfloat16 [2, 256, 1024, 320], P(None, ('group', 'row'), 'col'), may hold values from -6 to 6
- first_mean: float32 [32], replicated, may hold values from -2 to 2
- first_scale: float32 [32], replicated, may hold values from 0.5 to 2
- first_gain: float32 [320], replicated, may hold values from 0.1 to 1.9
- first_shift: float32 [320], replicated, may hold values from -3 to 3
- first_kernel: bfloat16 [3, 3, 320, 320], replicated, may hold values from -0.109375 to 0.109375
- first_bias: float32 [320], replicated, may hold values from -3 to 3
- branch_mean: float32 [2, 32], replicated, may hold values from -2 to 2
- branch_scale: float32 [2, 32], replicated, may hold values from 0.5 to 2
- branch_gain: float32 [2, 320], replicated, may hold values from 0.1 to 1.9
- branch_shift: float32 [2, 320], replicated, may hold values from -3 to 3
- branch_kernel: bfloat16 [2, 3, 3, 320, 320], replicated, may hold values from -0.109375 to 0.109375
- branch_bias: float32 [2, 320], replicated, may hold values from -3 to 3
- proj_weight: bfloat16 [2, 320, 320], replicated, may hold values from -0.3125 to 0.3125
- proj_bias: float32 [2, 320], replicated, may hold values from -3 to 3
- second_mean: float32 [32], replicated, may hold values from -2 to 2
- second_scale: float32 [32], replicated, may hold values from 0.3 to 1.2
- second_gain: float32 [320], replicated, may hold values from 0.1 to 1.9
- second_shift: float32 [320], replicated, may hold values from -3 to 3
- second_kernel: bfloat16 [3, 3, 320, 320], replicated, may hold values from -0.109375 to 0.109375
- second_bias: float32 [320], replicated, may hold values from -3 to 3
Outputs:
- blended: bfloat16 [256, 1024, 320], P('group', ('col', 'row'))
The draws below stay inside these ranges and needn't reach their ends.
All inputs are finite; a program needn't handle non-finite values.
Results may differ from the reference program's by a relative error of at most 0.0057.
Values may be sent and summed in bfloat16 or wider, within the bound.
A program may use at most 128 MiB of HBM per device.

```python
import math
import jax
import jax.numpy as jnp
from jax import lax

C = 320
G = 32
H = 256
W = 1024


def levels(stream_key, extent, cuts, least, top_value):
    def one(dim, parts):
        heights = jax.random.uniform(jax.random.fold_in(jax.random.fold_in(stream_key, 6), dim), (parts,), jnp.float32, least / len(cuts), top_value / len(cuts))
        return jnp.repeat(jnp.exp(heights), extent[dim] // parts).reshape((-1,) + (1,) * (len(extent) - dim - 1))

    factor_of = one(*cuts[0])
    for cut in cuts[1:]:
        factor_of = factor_of * one(*cut)
    return factor_of


def bell_draw(rng, extent, scale, most, shards=(), dtype=jnp.bfloat16):
    level = levels(rng, extent, shards, -0.22, 0.18) if shards else 1.0
    values = jax.random.normal(rng, extent, jnp.float32) * scale * level
    return jnp.minimum(jnp.maximum(values, -most), most).astype(dtype)


def setup_inputs(seed: int = 0) -> dict:
    key_of = jax.random.split(jax.random.key(seed), 23)
    return {
        "latent": bell_draw(key_of[0], (H, W, C), 1.0, 6.0, ((0, 4), (1, 32))),
        "control": bell_draw(key_of[1], (2, H, W, C), 1.0, 6.0, ((1, 16), (2, 8))),
        "first_mean": bell_draw(key_of[2], (G,), 0.3, 2.0, (), jnp.float32),
        "first_scale": jnp.clip(jnp.exp(jax.random.uniform(key_of[3], (G,), jnp.float32, math.log(0.5), math.log(2.0))), 0.5, 2.0),
        "first_gain": jnp.clip(1.0 + 0.18 * jax.random.normal(key_of[4], (C,), jnp.float32), 0.1, 1.9),
        "first_shift": bell_draw(key_of[5], (C,), 0.5, 3.0, (), jnp.float32),
        "first_kernel": bell_draw(key_of[6], (3, 3, C, C), (9 * C) ** -0.5, 0.109375),
        "first_bias": bell_draw(key_of[7], (C,), 0.5, 3.0, (), jnp.float32),
        "branch_mean": bell_draw(key_of[8], (2, G), 0.3, 2.0, (), jnp.float32),
        "branch_scale": jnp.clip(jnp.exp(jax.random.uniform(key_of[9], (2, G), jnp.float32, math.log(0.5), math.log(2.0))), 0.5, 2.0),
        "branch_gain": jnp.clip(1.0 + 0.18 * jax.random.normal(key_of[10], (2, C), jnp.float32), 0.1, 1.9),
        "branch_shift": bell_draw(key_of[11], (2, C), 0.5, 3.0, (), jnp.float32),
        "branch_kernel": bell_draw(key_of[12], (2, 3, 3, C, C), (9 * C) ** -0.5, 0.109375),
        "branch_bias": bell_draw(key_of[13], (2, C), 0.5, 3.0, (), jnp.float32),
        "proj_weight": bell_draw(key_of[14], (2, C, C), C ** -0.5, 0.3125),
        "proj_bias": bell_draw(key_of[15], (2, C), 0.5, 3.0, (), jnp.float32),
        "second_mean": bell_draw(key_of[16], (G,), 0.3, 2.0, (), jnp.float32),
        "second_scale": jnp.clip(jnp.exp(jax.random.uniform(key_of[17], (G,), jnp.float32, math.log(0.3), math.log(1.2))), 0.3, 1.2),
        "second_gain": jnp.clip(1.0 + 0.18 * jax.random.normal(key_of[18], (C,), jnp.float32), 0.1, 1.9),
        "second_shift": bell_draw(key_of[19], (C,), 0.5, 3.0, (), jnp.float32),
        "second_kernel": bell_draw(key_of[20], (3, 3, C, C), (9 * C) ** -0.5, 0.109375),
        "second_bias": bell_draw(key_of[21], (C,), 0.5, 3.0, (), jnp.float32),
    }


def widen(stat, width):
    return jnp.repeat(stat, width // stat.shape[-1], axis=-1)


def activate(value, mean, scale, gain, shift):
    width = value.shape[-1]
    normed = (value.astype(jnp.float32) - widen(mean, width)) * widen(scale, width) * gain + shift
    return jax.nn.silu(normed).astype(jnp.bfloat16)


def convolve(image, kernel, bias):
    rows, cols, width = image.shape
    padded = jnp.pad(image, ((1, 1), (1, 1), (0, 0)))
    total = jnp.zeros((rows * cols, kernel.shape[-1]), jnp.float32)
    for offset_y in range(3):
        for offset_x in range(3):
            piece = padded[offset_y:offset_y + rows, offset_x:offset_x + cols].reshape(rows * cols, width)
            total = total + jnp.dot(piece, kernel[offset_y, offset_x], preferred_element_type=jnp.float32)
    return (total + bias).reshape(rows, cols, -1)


def reference(latent, control, first_mean, first_scale, first_gain, first_shift, first_kernel, first_bias,
              branch_mean, branch_scale, branch_gain, branch_shift, branch_kernel, branch_bias,
              proj_weight, proj_bias, second_mean, second_scale, second_gain, second_shift,
              second_kernel, second_bias):
    rows, cols, width = latent.shape
    first_act = activate(latent, first_mean, first_scale, first_gain, first_shift)
    hidden = convolve(first_act, first_kernel, first_bias)
    summed = jnp.zeros((rows * cols, width), jnp.float32)
    for branch in range(2):
        branch_act = activate(control[branch], branch_mean[branch], branch_scale[branch],
                              branch_gain[branch], branch_shift[branch])
        feature = convolve(branch_act, branch_kernel[branch], branch_bias[branch]).astype(jnp.bfloat16)
        summed = summed + jnp.dot(feature.reshape(rows * cols, width), proj_weight[branch],
                                  preferred_element_type=jnp.float32) + proj_bias[branch]
    residual = lax.optimization_barrier(summed.astype(jnp.bfloat16)).reshape(rows, cols, width)
    second_act = activate(hidden, second_mean, second_scale, second_gain, second_shift)
    result = latent.astype(jnp.float32) + convolve(second_act, second_kernel, second_bias) + residual.astype(jnp.float32)
    return result.astype(jnp.bfloat16)
```

```python
import functools

import jax
import jax.numpy as jnp
from jax import lax
from jax.experimental import pallas as pl
from jax.experimental.pallas import tpu as pltpu
from jax.sharding import PartitionSpec as P

MESH = pl.DeviceIdType.MESH
F32 = jnp.float32
BF16 = jnp.bfloat16
DIRS = [(i, j) for i in (-1, 0, 1) for j in (-1, 0, 1) if (i, j) != (0, 0)]
C = 320
FIRST, BRANCH, SECOND, BIAS = 0, 2, 6, 8
CROWS, CCOLS, CSTRIDE = 16, 128, 144
BROWS, BCOLS, BSTRIDE = 64, 32, 48
PART = 4


def swish(value, table, at):
    half = value * table[at : at + 1, :] + table[at + 1 : at + 2, :]
    return half + half * jnp.tanh(half)


def tiles(value):
    return value[..., 0:128], value[..., 128:256], value[..., 256:320]


class Tiling:
    def __init__(self, mesh_sizes, kind):
        g, c, r = (lax.axis_index(a) for a in ("group", "col", "row"))
        ng, nc, nr = mesh_sizes
        self.nr = nr
        self.kind = kind
        if kind == "branch":
            self.row, self.col, self.rows, self.cols = g * nr + r, c, ng * nr, nc
        else:
            self.row, self.col, self.rows, self.cols = g, c * nr + r, ng, nc * nr

    def at(self, i, j):
        row, col = self.row + i, self.col + j
        if self.kind == "branch":
            return (row // self.nr, col, lax.rem(row, self.nr))
        return (row, col // self.nr, lax.rem(col, self.nr))

    def has(self, i, j):
        row, col = self.row + i, self.col + j
        return (row >= 0) & (row < self.rows) & (col >= 0) & (col < self.cols)


class Halo:
    def __init__(self, tiling, image, rows, cols, bufs):
        self.tiling, self.image, self.rows, self.cols = tiling, image, rows, cols
        self.srow, self.scol, self.scor, self.rrow, self.rcol, self.rcor, self.ss, self.rs = bufs
        self.planes = image.shape[0]
        self.stride = image.shape[2]
        self.flat = image.reshape(self.planes, image.shape[1] * self.stride, 128)

    def slot(self, i, j, bufs):
        row, col, cor = bufs
        if j == 0:
            return row.at[(i + 1) // 2]
        if i == 0:
            return col.at[(j + 1) // 2]
        return cor.at[(i + 1) + (j + 1) // 2]

    def copy(self, i, j):
        n = DIRS.index((i, j))
        return pltpu.make_async_remote_copy(
            src_ref=self.slot(i, j, (self.srow, self.scol, self.scor)),
            dst_ref=self.slot(i, j, (self.rrow, self.rcol, self.rcor)),
            send_sem=self.ss.at[n],
            recv_sem=self.rs.at[n],
            device_id=self.tiling.at(i, j),
            device_id_type=MESH,
        )

    def clear(self):
        for i, j in DIRS:

            @pl.when(jnp.logical_not(self.tiling.has(-i, -j)))
            def _():
                slot = self.slot(i, j, (self.rrow, self.rcol, self.rcor))
                slot[...] = jnp.zeros(slot.shape, slot.dtype)

    def send(self):
        edge_row = {-1: 1, 1: self.rows}
        edge_col = {-1: 8, 1: 7 + self.cols}
        for p in range(self.planes):
            for i in (-1, 1):
                self.srow[(i + 1) // 2, p] = self.image[
                    p, edge_row[i], 8 : 8 + self.cols, :
                ].astype(BF16)
            for j in (-1, 1):
                self.scol[(j + 1) // 2, p] = self.flat[
                    p, pl.ds(self.stride + edge_col[j], self.rows, stride=self.stride), :
                ].astype(BF16)
            for i in (-1, 1):
                for j in (-1, 1):
                    pixel = self.image[p, edge_row[i], edge_col[j] : edge_col[j] + 1, :]
                    self.scor[(i + 1) + (j + 1) // 2, p] = jnp.broadcast_to(
                        pixel, (16, 128)
                    ).astype(BF16)
        for i, j in DIRS:

            @pl.when(self.tiling.has(i, j))
            def _():
                self.copy(i, j).start()

    def receive(self):
        for i, j in DIRS:

            @pl.when(self.tiling.has(-i, -j))
            def _():
                self.copy(i, j).wait_recv()

        halo_row = {1: 0, -1: self.rows + 1}
        halo_col = {1: 7, -1: 8 + self.cols}
        for p in range(self.planes):
            for i in (-1, 1):
                self.image[p, halo_row[i], 8 : 8 + self.cols, :] = self.rrow[
                    (i + 1) // 2, p
                ].astype(F32)
            for j in (-1, 1):
                self.flat[
                    p, pl.ds(self.stride + halo_col[j], self.rows, stride=self.stride), :
                ] = self.rcol[(j + 1) // 2, p].astype(F32)
            for i in (-1, 1):
                for j in (-1, 1):
                    self.image[p, halo_row[i], halo_col[j] : halo_col[j] + 1, :] = self.rcor[
                        (i + 1) + (j + 1) // 2, p
                    ].astype(F32)[0:1]

    def finish(self):
        for i, j in DIRS:

            @pl.when(self.tiling.has(i, j))
            def _():
                self.copy(i, j).wait_send()


def spread(image, plane, row, cols):
    parts = []
    for start in (7, 8, 9):
        for t in range(2):
            parts.append(image[plane + t, row, start : start + cols, :].astype(BF16))
    rest = [
        image[plane + 2, row, start : start + cols, :].astype(BF16)[:, 0:64] for start in (7, 8, 9)
    ]
    parts.append(jnp.concatenate([rest[0], rest[1]], axis=1))
    parts.append(jnp.concatenate([rest[2], jnp.zeros((cols, 64), BF16)], axis=1))
    return jnp.concatenate(parts, axis=1)


def kernel(
    sizes,
    latent_hbm,
    control_hbm,
    table,
    first_hbm,
    branch_hbm,
    second_hbm,
    proj_hbm,
    out_ref,
    latent,
    control,
    main_w,
    rest_w,
    stage_w,
    proj_w,
    cimage,
    bimage,
    cspread,
    bspread,
    crest,
    brest,
    outer,
    send,
    got,
    *more,
):
    halo_bufs = [more[0:8], more[8:16], more[16:24]]
    load_sem, weight_sem, res_send, res_recv = more[24:]
    g, c, r = (lax.axis_index(a) for a in ("group", "col", "row"))
    nr = sizes[2]
    ctile, btile = Tiling(sizes, "branch"), Tiling(sizes, "base")

    barrier = pltpu.get_barrier_semaphore()
    count = nr - 1
    for tile in (ctile, btile):
        for i, j in DIRS:
            there = tile.has(i, j)
            count = count + there.astype(jnp.int32)

            @pl.when(there)
            def _():
                pl.semaphore_signal(
                    barrier, inc=1, device_id=tile.at(i, j), device_id_type=MESH
                )

    def peer(step):
        return (lax.rem(r + 2, 4), lax.rem(r // 2 + 1, 2) * 2 + 1 - lax.rem(r, 2),
                (r // 2) * 2 + 1 - lax.rem(r, 2))[step]

    for step in range(3):
        pl.semaphore_signal(barrier, inc=1, device_id=(g, c, peer(step)), device_id_type=MESH)

    control_load = pltpu.make_async_copy(control_hbm, control, load_sem.at[0])
    control_load.start()
    latent_load = pltpu.make_async_copy(latent_hbm, latent, load_sem.at[1])
    latent_load.start()
    proj_load = pltpu.make_async_copy(proj_hbm, proj_w, load_sem.at[2])
    weight_loads = []
    for n, ref in enumerate(
        (branch_hbm.at[0], branch_hbm.at[1], first_hbm, second_hbm)
    ):
        weight_loads.append(pltpu.make_async_copy(ref, stage_w.at[n], weight_sem.at[n]))
    for load in weight_loads[:2] + [proj_load] + weight_loads[2:]:
        load.start()

    chalo = Halo(ctile, cimage, CROWS, CCOLS, halo_bufs[0])
    bhalo = Halo(btile, bimage, BROWS, BCOLS, halo_bufs[1])
    hhalo = Halo(btile, bimage, BROWS, BCOLS, halo_bufs[2])

    control_load.wait()
    for branch in range(2):

        def act_control(row, _):
            value = swish(
                control[branch, row].astype(F32), table, BRANCH + 2 * branch
            )
            for t, piece in enumerate(tiles(value)):
                cimage[3 * branch + t, row + 1, 8 : 8 + CCOLS, 0 : piece.shape[1]] = piece
            return 0

        lax.fori_loop(0, CROWS, act_control, 0)
    pl.semaphore_wait(barrier, count)
    chalo.send()

    latent_load.wait()

    def act_latent(n, _):
        rows = pl.ds(n * 4, 4)
        value = swish(latent[rows].astype(F32).reshape(4 * BCOLS, C), table, FIRST)
        for t, piece in enumerate(tiles(value)):
            bimage[t, pl.ds(n * 4 + 1, 4), 8 : 8 + BCOLS, 0 : piece.shape[1]] = piece.reshape(
                4, BCOLS, piece.shape[1]
            )
        return 0

    lax.fori_loop(0, BROWS // 4, act_latent, 0)
    bhalo.send()
    chalo.clear()
    bhalo.clear()
    hhalo.clear()

    def arrange(n):
        weight_loads[n].wait()

        def tap_column(dx, _):
            low, high = stage_w.at[n, :, :, 0:256], stage_w.at[n, :, :, 256:320]
            for dy in range(3):
                main_w[n, dy, pl.ds(dx * 256, 256), :] = stage_w[n, dy, dx, 0:256, 0:256]
                main_w[n, dy, pl.ds(768 + dx * 64, 64), :] = stage_w[n, dy, dx, 256:320, 0:256]
            for at, start, size in ((dx * 256, 0, 256), (768 + dx * 64, 256, 64)):
                pieces = [stage_w[n, dy, dx, start : start + size, 256:320] for dy in range(3)]
                rest_w[n, pl.ds(at, size), :] = jnp.concatenate(
                    pieces + [jnp.zeros((size, 64), BF16)], axis=1
                )
            return 0

        lax.fori_loop(0, 3, tap_column, 0)
        for dy in range(3):
            main_w[n, dy, 960:1024, :] = jnp.zeros((64, 256), BF16)
        rest_w[n, 960:1024, :] = jnp.zeros((64, 256), BF16)

    for n in range(4):
        arrange(n)
    proj_load.wait()

    chalo.receive()
    for branch in range(2):

        def spread_control(row, _):
            cspread[branch, row] = spread(cimage, 3 * branch, row, CCOLS)
            return 0

        lax.fori_loop(0, CROWS + 2, spread_control, 0)

        def rest_control(n, _):
            rows = pl.ds(n * 6, 6)
            crest[branch, rows] = jnp.dot(
                cspread[branch, rows].reshape(6 * CCOLS, 1024),
                rest_w[branch],
                preferred_element_type=F32,
            ).reshape(6, CCOLS, 256)
            return 0

        lax.fori_loop(0, 3, rest_control, 0)

    def feature(branch, row):
        wide = jnp.concatenate(
            [
                cspread[branch, pl.ds(row + dy, PART)].reshape(PART * CCOLS, 1024)
                for dy in range(3)
            ],
            axis=1,
        )
        main = jnp.dot(wide, main_w[branch].reshape(3072, 256), preferred_element_type=F32)
        rest = (
            crest[branch, pl.ds(row, PART), :, 0:64]
            + crest[branch, pl.ds(row + 1, PART), :, 64:128]
            + crest[branch, pl.ds(row + 2, PART), :, 128:192]
        ).reshape(PART * CCOLS, 64)
        bias = table[BIAS + branch : BIAS + branch + 1, :]
        return (main + bias[:, 0:256]).astype(BF16), (rest + bias[:, 256:320]).astype(BF16)

    def res_copy(step, part):
        q = peer(step)
        return pltpu.make_async_remote_copy(
            src_ref=send.at[q, pl.ds(part * PART, PART)],
            dst_ref=got.at[pl.ds(r * CROWS + part * PART, PART)],
            send_sem=res_send.at[step, part],
            recv_sem=res_recv.at[step, part],
            device_id=(g, c, q),
            device_id_type=MESH,
        )

    def branch_part(part):
        row = part * PART
        m0, r0 = feature(0, row)
        m1, r1 = feature(1, row)
        both = jnp.concatenate([m0, m1, jnp.concatenate([r0, r1], axis=1)], axis=1)
        proj = jnp.concatenate(
            [
                proj_w[0, 0:256, :],
                proj_w[1, 0:256, :],
                proj_w[0, 256:320, :],
                proj_w[1, 256:320, :],
            ],
            axis=0,
        )
        residual = jnp.dot(both, proj, preferred_element_type=F32) + table[BIAS + 2 : BIAS + 3, :]
        residual = residual.astype(BF16).reshape(PART, CCOLS, C)
        for q in range(4):
            send[q, row : row + PART] = residual[:, q * BCOLS : (q + 1) * BCOLS, :]
        got[pl.ds(r * CROWS + row, PART)] = send[r, row : row + PART]
        for step in range(3):
            res_copy(step, part).start()

    def spread_base(n):
        def one(row, _):
            bspread[row] = spread(bimage, 0, row, BCOLS)
            return 0

        lax.fori_loop(0, BROWS + 2, one, 0)

        def rest(m, _):
            rows = pl.ds(m * 22, 22)
            brest[rows] = jnp.dot(
                bspread[rows].reshape(22 * BCOLS, 1024), rest_w[n], preferred_element_type=F32
            ).reshape(22, BCOLS, 256)
            return 0

        lax.fori_loop(0, 3, rest, 0)

    def conv_base(n, row, bias_at):
        wide = jnp.concatenate(
            [bspread[pl.ds(row + dy, 16)].reshape(16 * BCOLS, 1024) for dy in range(3)], axis=1
        )
        main = jnp.dot(wide, main_w[n].reshape(3072, 256), preferred_element_type=F32)
        rest = (
            brest[pl.ds(row, 16), :, 0:64]
            + brest[pl.ds(row + 1, 16), :, 64:128]
            + brest[pl.ds(row + 2, 16), :, 128:192]
        ).reshape(16 * BCOLS, 64)
        bias = table[bias_at : bias_at + 1, :]
        return jnp.concatenate([main, rest], axis=1) + bias

    branch_part(0)
    branch_part(1)

    bhalo.receive()
    spread_base(2)

    def first_conv(n, _):
        row = n * 16
        value = swish(conv_base(2, row, BIAS + 3), table, SECOND)
        for t, piece in enumerate(tiles(value)):
            bimage[t, pl.ds(row + 1, 16), 8 : 8 + BCOLS, 0 : piece.shape[1]] = piece.reshape(
                16, BCOLS, piece.shape[1]
            )
        return 0

    lax.fori_loop(0, 4, first_conv, 0)
    hhalo.send()

    branch_part(2)
    branch_part(3)

    hhalo.receive()
    spread_base(3)

    def second_conv(n, _):
        row = n * 16
        value = conv_base(3, row, BIAS + 4).reshape(16, BCOLS, C)
        outer[pl.ds(row, 16)] = value + latent[pl.ds(row, 16)].astype(F32)
        return 0

    lax.fori_loop(0, 4, second_conv, 0)

    for step in range(3):
        for part in range(4):
            res_copy(step, part).wait_recv()

    def add_residual(n, _):
        rows = pl.ds(n * 8, 8)
        out_ref[rows] = (outer[rows] + got[rows].astype(F32)).astype(BF16)
        return 0

    lax.fori_loop(0, BROWS // 8, add_residual, 0)
    for step in range(3):
        for part in range(4):
            res_copy(step, part).wait_send()
    for halo in (chalo, bhalo, hhalo):
        halo.finish()


def halo_scratch(planes, rows, cols):
    both = [
        pltpu.VMEM((2, planes, cols, 128), BF16),
        pltpu.VMEM((2, planes, rows, 128), BF16),
        pltpu.VMEM((4, planes, 16, 128), BF16),
    ]
    return both + both + [pltpu.SemaphoreType.DMA((8,)), pltpu.SemaphoreType.DMA((8,))]


def body(
    sizes,
    latent,
    control,
    first_mean,
    first_scale,
    first_gain,
    first_shift,
    first_kernel,
    first_bias,
    branch_mean,
    branch_scale,
    branch_gain,
    branch_shift,
    branch_kernel,
    branch_bias,
    proj_weight,
    proj_bias,
    second_mean,
    second_scale,
    second_gain,
    second_shift,
    second_kernel,
    second_bias,
):
    mean = jnp.concatenate([first_mean[None], branch_mean, second_mean[None]])
    scale = jnp.concatenate([first_scale[None], branch_scale, second_scale[None]])
    gain = jnp.concatenate([first_gain[None], branch_gain, second_gain[None]])
    shift = jnp.concatenate([first_shift[None], branch_shift, second_shift[None]])
    slope = 0.5 * (jnp.repeat(scale, C // scale.shape[1], axis=1) * gain)
    offset = 0.5 * shift - jnp.repeat(mean, C // mean.shape[1], axis=1) * slope
    norms = jnp.stack([slope, offset], axis=1).reshape(8, C)
    table = jnp.concatenate(
        [
            norms,
            branch_bias,
            jnp.sum(proj_bias, axis=0, keepdims=True),
            first_bias[None],
            second_bias[None],
            jnp.zeros((3, C), F32),
        ]
    )
    hbm = pl.BlockSpec(memory_space=pl.ANY)
    vmem = pl.BlockSpec(memory_space=pltpu.VMEM)
    return pl.pallas_call(
        functools.partial(kernel, sizes),
        out_shape=jax.ShapeDtypeStruct((BROWS, BCOLS, C), BF16),
        in_specs=[hbm, hbm, vmem, hbm, hbm, hbm, hbm],
        out_specs=vmem,
        scratch_shapes=[
            pltpu.VMEM((BROWS, BCOLS, C), BF16),
            pltpu.VMEM((2, CROWS, CCOLS, C), BF16),
            pltpu.VMEM((4, 3, 1024, 256), BF16),
            pltpu.VMEM((4, 1024, 256), BF16),
            pltpu.VMEM((4, 3, 3, C, C), BF16),
            pltpu.VMEM((2, C, C), BF16),
            pltpu.VMEM((6, CROWS + 2, CSTRIDE, 128), F32),
            pltpu.VMEM((3, BROWS + 2, BSTRIDE, 128), F32),
            pltpu.VMEM((2, CROWS + 2, CCOLS, 1024), BF16),
            pltpu.VMEM((BROWS + 2, BCOLS, 1024), BF16),
            pltpu.VMEM((2, CROWS + 2, CCOLS, 256), F32),
            pltpu.VMEM((BROWS + 2, BCOLS, 256), F32),
            pltpu.VMEM((BROWS, BCOLS, C), F32),
            pltpu.VMEM((4, CROWS, BCOLS, C), BF16),
            pltpu.VMEM((BROWS, BCOLS, C), BF16),
        ]
        + halo_scratch(6, CROWS, CCOLS)
        + halo_scratch(3, BROWS, BCOLS)
        + halo_scratch(3, BROWS, BCOLS)
        + [
            pltpu.SemaphoreType.DMA((3,)),
            pltpu.SemaphoreType.DMA((4,)),
            pltpu.SemaphoreType.DMA((3, 4)),
            pltpu.SemaphoreType.DMA((3, 4)),
        ],
        compiler_params=pltpu.CompilerParams(
            collective_id=0, has_side_effects=True, vmem_limit_bytes=67_000_000
        ),
    )(latent, control, table, first_kernel, branch_kernel, second_kernel, proj_weight)


def solution(mesh):
    sizes = (mesh.shape["group"], mesh.shape["col"], mesh.shape["row"])
    in_specs = (
        P("group", ("col", "row"), None),
        P(None, ("group", "row"), "col", None),
    ) + (P(),) * 20
    out_specs = P("group", ("col", "row"), None)
    return jax.shard_map(
        functools.partial(body, sizes),
        mesh=mesh,
        in_specs=in_specs,
        out_specs=out_specs,
        check_vma=False,
    )
```

```python
import functools

import jax
import jax.numpy as jnp
from jax import lax
from jax.experimental import pallas as pl
from jax.experimental.pallas import tpu as pltpu
from jax.sharding import PartitionSpec as P

MESH = pl.DeviceIdType.MESH
F32 = jnp.float32
BF16 = jnp.bfloat16
DIRS = [(i, j) for i in (-1, 0, 1) for j in (-1, 0, 1) if (i, j) != (0, 0)]
C = 320
FIRST, BRANCH, SECOND, BIAS = 0, 2, 6, 8
CROWS, CCOLS = 16, 128
BROWS, BCOLS = 64, 32
BLOCK, STRIDE = 128, 144
PART = 4
CHUNK = 16


def swish(value, table, at):
    half = value * table[at : at + 1, :] + table[at + 1 : at + 2, :]
    return half + half * jnp.tanh(half)


def widen(stat):
    groups = stat.shape[1]
    across = lax.broadcasted_iota(jnp.int32, (groups, groups), 0)
    along = lax.broadcasted_iota(jnp.int32, (groups, groups), 1)
    column = jnp.sum(
        jnp.where(across == along, jnp.broadcast_to(stat, (groups, groups)), 0.0),
        axis=1,
        keepdims=True,
    )
    first = lax.broadcasted_iota(jnp.int32, (groups, C), 0) * (C // groups)
    channel = lax.broadcasted_iota(jnp.int32, (groups, C), 1)
    inside = (channel >= first) & (channel < first + C // groups)
    return jnp.sum(
        jnp.where(inside, jnp.broadcast_to(column, (groups, C)), 0.0), axis=0, keepdims=True
    )


class Tiling:
    def __init__(self, mesh_sizes, kind):
        g, c, r = (lax.axis_index(a) for a in ("group", "col", "row"))
        ng, nc, nr = mesh_sizes
        self.nr = nr
        self.kind = kind
        if kind == "branch":
            self.row, self.col, self.rows, self.cols = g * nr + r, c, ng * nr, nc
        else:
            self.row, self.col, self.rows, self.cols = g, c * nr + r, ng, nc * nr

    def at(self, i, j):
        row, col = self.row + i, self.col + j
        if self.kind == "branch":
            return (row // self.nr, col, lax.rem(row, self.nr))
        return (row, col // self.nr, lax.rem(col, self.nr))

    def has(self, i, j):
        row, col = self.row + i, self.col + j
        return (row >= 0) & (row < self.rows) & (col >= 0) & (col < self.cols)


class Halo:
    def __init__(self, tiling, image, rows, cols, bufs):
        self.tiling, self.image, self.rows, self.cols = tiling, image, rows, cols
        self.srow, self.scol, self.scor, self.rrow, self.rcol, self.rcor, self.ss, self.rs = bufs
        self.planes = image.shape[0]
        self.per = BLOCK // cols
        self.blocks = rows // self.per
        self.flat = image.reshape(self.planes, image.shape[1] * STRIDE, 128)

    def slot(self, i, j, bufs):
        row, col, cor = bufs
        if j == 0:
            return row.at[(i + 1) // 2]
        if i == 0:
            return col.at[(j + 1) // 2]
        return cor.at[(i + 1) + (j + 1) // 2]

    def copy(self, i, j):
        n = DIRS.index((i, j))
        return pltpu.make_async_remote_copy(
            src_ref=self.slot(i, j, (self.srow, self.scol, self.scor)),
            dst_ref=self.slot(i, j, (self.rrow, self.rcol, self.rcor)),
            send_sem=self.ss.at[n],
            recv_sem=self.rs.at[n],
            device_id=self.tiling.at(i, j),
            device_id_type=MESH,
        )

    def clear(self):
        for i, j in DIRS:

            @pl.when(jnp.logical_not(self.tiling.has(-i, -j)))
            def _():
                slot = self.slot(i, j, (self.rrow, self.rcol, self.rcor))
                slot[...] = jnp.zeros(slot.shape, slot.dtype)

    def send(self):
        cols, blocks = self.cols, self.blocks
        edge = {-1: (0, 8), 1: (blocks - 1, 8 + BLOCK - cols)}
        for p in range(self.planes):
            for i in (-1, 1):
                block, at = edge[i]
                self.srow[(i + 1) // 2, p] = self.image[p, block, at : at + cols, :].astype(BF16)
                for j in (-1, 1):
                    pixel = at + (cols - 1) * ((j + 1) // 2)
                    self.scor[(i + 1) + (j + 1) // 2, p] = jnp.broadcast_to(
                        self.image[p, block, pixel : pixel + 1, :], (16, 128)
                    ).astype(BF16)
            for j in (-1, 1):
                for inner in range(self.per):
                    start = 8 + inner * cols + (cols - 1) * ((j + 1) // 2)
                    self.scol[(j + 1) // 2, p, inner * blocks : (inner + 1) * blocks] = self.flat[
                        p, pl.ds(start, blocks, stride=STRIDE), :
                    ].astype(BF16)
        for i, j in DIRS:

            @pl.when(self.tiling.has(i, j))
            def _():
                self.copy(i, j).start()

    def receive(self, targets, sides):
        cols, blocks = self.cols, self.blocks
        for i, j in DIRS:

            @pl.when(self.tiling.has(-i, -j))
            def _():
                self.copy(i, j).wait_recv()

        for n, target in enumerate(targets):
            for i in (-1, 1):
                for t in range(3):
                    p = 3 * n + t
                    self.image[p, blocks, 8 : 8 + cols, :] = self.rrow[(i + 1) // 2, p].astype(F32)
                    for j, at in ((1, 7), (-1, 8 + cols)):
                        self.image[p, blocks, at : at + 1, :] = self.rcor[
                            (i + 1) + (j + 1) // 2, p
                        ].astype(F32)[0:1]
                row = 0 if i == 1 else self.rows + 1
                spread(self.image, 3 * n, blocks, cols, target.at[pl.ds(row, 1)])
            for j in (-1, 1):
                for t in range(3):
                    sides[(j + 1) // 2, t, 0 : self.rows // 8] = (
                        self.rcol[(j + 1) // 2, 3 * n + t]
                        .astype(F32)
                        .reshape(self.rows // 8, 8, 128)
                    )
            sub = lax.broadcasted_iota(jnp.int32, (16, 128), 0)
            lane = lax.broadcasted_iota(jnp.int32, (16, 128), 1)
            places = (
                (1, 0, 0, False),
                (1, 1, 128, False),
                (1, 2, 768, True),
                (0, 0, 512, False),
                (0, 1, 640, False),
                (0, 2, 896, True),
            )

            def fix(group, _):
                for s in range(8):
                    k = group * 8 + s
                    row = lax.rem(k, blocks) * self.per + k // blocks + 1
                    for side, t, lanes, leftover in places:
                        edge = (sub == 0) if side == 1 else (sub == 15)
                        if leftover:
                            edge = edge & (lane < 64)
                        at = 0 if side == 1 else cols - 16
                        pixel = jnp.broadcast_to(sides[side, t, group, s : s + 1, :], (16, 128))
                        held = target[row, at : at + 16, lanes : lanes + 128]
                        target[row, at : at + 16, lanes : lanes + 128] = jnp.where(
                            edge, pixel, held.astype(F32)
                        ).astype(BF16)
                return 0

            lax.fori_loop(0, self.rows // 8, fix, 0)

    def finish(self):
        for i, j in DIRS:

            @pl.when(self.tiling.has(i, j))
            def _():
                self.copy(i, j).wait_send()


def place(image, plane, block, value):
    image[plane, block, 8 : 8 + BLOCK, :] = value[:, 0:128]
    image[plane + 1, block, 8 : 8 + BLOCK, :] = value[:, 128:256]
    image[plane + 2, block, 8 : 8 + BLOCK, 0:64] = value[:, 256:320]


def spread(image, plane, block, cols, target):
    rows = target.shape[0]
    size = rows * cols
    rest = []
    for n, start in enumerate((7, 8, 9)):
        for t in range(2):
            piece = image[plane + t, block, start : start + size, :].astype(BF16)
            lanes = n * 256 + t * 128
            target[:, :, lanes : lanes + 128] = piece.reshape(rows, cols, 128)
        rest.append(image[plane + 2, block, start : start + size, :][:, 0:64])
    for lanes, pair in ((768, rest[0:2]), (896, [rest[2], jnp.zeros((size, 64), F32)])):
        piece = jnp.concatenate(pair, axis=1).astype(BF16)
        target[:, :, lanes : lanes + 128] = piece.reshape(rows, cols, 128)


def kernel(
    sizes,
    latent_hbm,
    control_hbm,
    first_hbm,
    branch_hbm,
    second_hbm,
    proj_hbm,
    first_mean,
    first_scale,
    first_gain,
    first_shift,
    first_bias,
    branch_mean,
    branch_scale,
    branch_gain,
    branch_shift,
    branch_bias,
    proj_bias,
    second_mean,
    second_scale,
    second_gain,
    second_shift,
    second_bias,
    out_ref,
    table,
    latent,
    control,
    main_w,
    tail_w,
    rest_w,
    stage_w,
    proj_w,
    cimage,
    bimage,
    cspread,
    bspread,
    hspread,
    crest,
    outer,
    send,
    got,
    sides,
    *more,
):
    halo_bufs = [more[0:8], more[8:16], more[16:24]]
    load_sem, weight_sem, res_send, res_recv = more[24:]
    g, c, r = (lax.axis_index(a) for a in ("group", "col", "row"))
    nr = sizes[2]
    ctile, btile = Tiling(sizes, "branch"), Tiling(sizes, "base")

    control_loads = [
        pltpu.make_async_copy(control_hbm.at[k], control.at[k], load_sem.at[k]) for k in range(2)
    ]
    for load in control_loads:
        load.start()

    barrier = pltpu.get_barrier_semaphore()
    count = nr - 1
    for tile in (ctile, btile):
        for i, j in DIRS:
            there = tile.has(i, j)
            count = count + there.astype(jnp.int32)

            @pl.when(there)
            def _():
                pl.semaphore_signal(
                    barrier, inc=1, device_id=tile.at(i, j), device_id_type=MESH
                )

    def peer(step):
        far = lax.rem(r // 2 + 1, 2) * 2
        core = lax.rem(r, 2)
        return (far + core, far + 1 - core, (r // 2) * 2 + 1 - core)[step]

    for step in range(3):
        pl.semaphore_signal(barrier, inc=1, device_id=(g, c, peer(step)), device_id_type=MESH)

    chalo = Halo(ctile, cimage, CROWS, CCOLS, halo_bufs[0])
    bhalo = Halo(btile, bimage, BROWS, BCOLS, halo_bufs[1])
    hhalo = Halo(btile, bimage, BROWS, BCOLS, halo_bufs[2])

    norms = ((first_mean, first_scale, first_gain, first_shift, 0),) + tuple(
        (branch_mean, branch_scale, branch_gain, branch_shift, k) for k in range(2)
    ) + ((second_mean, second_scale, second_gain, second_shift, 0),)

    def vector(ref, k):
        return ref[...].reshape(1, -1) if len(ref.shape) == 1 else ref[k : k + 1, :]

    for n, (*stats, k) in enumerate(norms):
        mean, scale, gain, shift = (vector(ref, k) for ref in stats)
        slope = 0.5 * (widen(scale) * gain)
        table[2 * n : 2 * n + 1, :] = slope
        table[2 * n + 1 : 2 * n + 2, :] = 0.5 * shift - widen(mean) * slope
    table[BIAS : BIAS + 2, :] = branch_bias[...]
    table[BIAS + 2 : BIAS + 3, :] = proj_bias[0:1, :] + proj_bias[1:2, :]
    table[BIAS + 3 : BIAS + 4, :] = vector(first_bias, 0)
    table[BIAS + 4 : BIAS + 5, :] = vector(second_bias, 0)

    for load in control_loads:
        load.wait()
    latent_load = pltpu.make_async_copy(latent_hbm, latent, load_sem.at[2])
    proj_load = pltpu.make_async_copy(proj_hbm, proj_w, load_sem.at[3])

    def weight_loads(n):
        ref = (branch_hbm.at[0], branch_hbm.at[1], first_hbm, second_hbm)[n]
        return (
            pltpu.make_async_copy(
                ref.at[:, :, 0:256, 0:256], main_w.at[n], weight_sem.at[n, 0]
            ),
            pltpu.make_async_copy(
                ref.at[:, :, 256:320, 0:256], tail_w.at[n, :, 0:3], weight_sem.at[n, 1]
            ),
            pltpu.make_async_copy(ref.at[:, :, :, 256:320], stage_w.at[n], weight_sem.at[n, 2]),
        )

    for load in (
        *weight_loads(0),
        *weight_loads(1),
        proj_load,
        latent_load,
        *weight_loads(2),
        *weight_loads(3),
    ):
        load.start()

    for branch in range(2):

        def act_control(n, _):
            for row in (2 * n, 2 * n + 1):
                value = swish(control[branch, row].T.astype(F32), table, BRANCH + 2 * branch)
                place(cimage, 3 * branch, row, value)
                spread(cimage, 3 * branch, row, CCOLS, cspread.at[branch, pl.ds(row + 1, 1)])
            return 0

        lax.fori_loop(0, CROWS // 2, act_control, 0)
    pl.semaphore_wait(barrier, count)
    chalo.send()
    chalo.clear()
    bhalo.clear()
    hhalo.clear()

    def arrange(n):
        for load in weight_loads(n):
            load.wait()

        def tap_column(dx, _):
            for at, start, size in ((dx * 256, 0, 256), (768 + dx * 64, 256, 64)):
                pieces = [stage_w[n, dy, dx, start : start + size, :] for dy in range(3)]
                rest_w[n, pl.ds(at, size), :] = jnp.concatenate(
                    pieces + [jnp.zeros((size, 64), BF16)], axis=1
                )
            return 0

        lax.fori_loop(0, 3, tap_column, 0)
        for dy in range(3):
            tail_w[n, dy, 3] = jnp.zeros((64, 256), BF16)
        rest_w[n, 960:1024, :] = jnp.zeros((64, 256), BF16)

    def main_dot(image_rows, n):
        weight = []
        for dy in range(3):
            weight += [main_w[n, dy].reshape(768, 256), tail_w[n, dy].reshape(256, 256)]
        return jnp.dot(
            jnp.concatenate(image_rows, axis=1),
            jnp.concatenate(weight, axis=0),
            preferred_element_type=F32,
        )

    def act_latent(n):
        value = swish(
            latent[pl.ds(n * 4, 4)].astype(F32).reshape(BLOCK, C), table, FIRST
        )
        place(bimage, 0, n, value)
        spread(bimage, 0, n, BCOLS, bspread.at[pl.ds(n * 4 + 1, 4)])

    def res_copy(step, part):
        q = peer(step)
        return pltpu.make_async_remote_copy(
            src_ref=send.at[q, part],
            dst_ref=got.at[r * 4 + part],
            send_sem=res_send.at[step, part],
            recv_sem=res_recv.at[step, part],
            device_id=(g, c, q),
            device_id_type=MESH,
        )

    def branch_part(part, beside=()):
        row = part * PART
        first, last = (0, PART + 2) if part == 0 else (row + 2, row + PART + 2)
        features = []
        for branch in range(2):
            for work in beside[branch::2]:
                act_latent(work)
            size = (last - first) * CCOLS
            crest[branch, first:last] = jnp.dot(
                cspread[branch, first:last].reshape(size, 1024),
                rest_w[branch],
                preferred_element_type=F32,
            ).reshape(last - first, CCOLS, 256)
            main = main_dot(
                [
                    cspread[branch, row + dy : row + dy + PART].reshape(PART * CCOLS, 1024)
                    for dy in range(3)
                ],
                branch,
            )
            rest = (
                crest[branch, row : row + PART, :, 0:64]
                + crest[branch, row + 1 : row + 1 + PART, :, 64:128]
                + crest[branch, row + 2 : row + 2 + PART, :, 128:192]
            ).reshape(PART * CCOLS, 64)
            bias = table[BIAS + branch : BIAS + branch + 1, :]
            features.append(
                ((main + bias[:, 0:256]).astype(BF16), (rest + bias[:, 256:320]).astype(BF16))
            )
        (m0, r0), (m1, r1) = features
        both = jnp.concatenate([m0, m1, jnp.concatenate([r0, r1], axis=1)], axis=1)
        proj = jnp.concatenate(
            [
                proj_w[0, 0:256, :],
                proj_w[1, 0:256, :],
                proj_w[0, 256:320, :],
                proj_w[1, 256:320, :],
            ],
            axis=0,
        )
        residual = jnp.dot(both, proj, preferred_element_type=F32) + table[BIAS + 2 : BIAS + 3, :]
        residual = residual.reshape(PART, CCOLS, C)
        for q in range(4):
            block = residual[:, q * BCOLS : (q + 1) * BCOLS, :].reshape(BLOCK, C)
            send[q, part, 0:128] = block[:, 0:128].astype(BF16)
            send[q, part, 128:256] = block[:, 128:256].astype(BF16)
            send[q, part, 256:320] = jnp.concatenate(
                [block[0:64, 256:320], block[64:128, 256:320]], axis=1
            ).astype(BF16)
        for step in range(3):
            res_copy(step, part).start()
        got[r * 4 + part] = send[r, part]

    def conv_base(n, image, row, bias_at):
        main = main_dot(
            [image[row + dy : row + dy + CHUNK].reshape(CHUNK * BCOLS, 1024) for dy in range(3)],
            n,
        )
        every = jnp.dot(
            image[row : row + CHUNK + 2].reshape((CHUNK + 2) * BCOLS, 1024),
            rest_w[n],
            preferred_element_type=F32,
        )
        size = CHUNK * BCOLS
        rest = (
            every[0:size, 0:64]
            + every[BCOLS : BCOLS + size, 64:128]
            + every[2 * BCOLS : 2 * BCOLS + size, 128:192]
        )
        bias = table[bias_at : bias_at + 1, :]
        return jnp.concatenate([main + bias[:, 0:256], rest + bias[:, 256:320]], axis=1)

    arrange(0)
    arrange(1)
    proj_load.wait()
    latent_load.wait()
    chalo.receive([cspread.at[0], cspread.at[1]], sides)
    branch_part(0, range(0, 8))
    branch_part(1, range(8, 16))
    bhalo.send()
    arrange(2)

    bhalo.receive([bspread], sides)
    for row in range(0, BROWS, CHUNK):
        value = swish(conv_base(2, bspread, row, BIAS + 3), table, SECOND)
        for k in range(CHUNK // 4):
            place(bimage, 0, row // 4 + k, value[k * BLOCK : (k + 1) * BLOCK])
            spread(
                bimage, 0, row // 4 + k, BCOLS, hspread.at[pl.ds(row + 4 * k + 1, 4)]
            )
    hhalo.send()

    branch_part(2)
    branch_part(3)
    arrange(3)

    hhalo.receive([hspread], sides)
    for row in range(0, BROWS, CHUNK):
        value = conv_base(3, hspread, row, BIAS + 4).reshape(CHUNK, BCOLS, C)
        outer[row : row + CHUNK] = value + latent[row : row + CHUNK].astype(F32)

    for step in range(3):
        for part in range(4):
            res_copy(step, part).wait_recv()

    def add_residual(n, _):
        rows = pl.ds(n * 4, 4)
        rest = got[n, 256:320]
        pieces = (
            got[n, 0:128],
            got[n, 128:256],
            jnp.concatenate([rest[:, 0:64], rest[:, 64:128]], axis=0),
        )
        for lanes, piece in zip((slice(0, 128), slice(128, 256), slice(256, 320)), pieces):
            total = outer[rows, :, lanes].reshape(BLOCK, -1) + piece.astype(F32)
            out_ref[rows, :, lanes] = total.astype(BF16).reshape(4, BCOLS, -1)
        return 0

    lax.fori_loop(0, BROWS // 4, add_residual, 0)
    for step in range(3):
        for part in range(4):
            res_copy(step, part).wait_send()
    for halo in (chalo, bhalo, hhalo):
        halo.finish()


def halo_scratch(planes, rows, cols):
    both = [
        pltpu.VMEM((2, planes, cols, 128), BF16),
        pltpu.VMEM((2, planes, rows, 128), BF16),
        pltpu.VMEM((4, planes, 16, 128), BF16),
    ]
    return both + both + [pltpu.SemaphoreType.DMA((8,)), pltpu.SemaphoreType.DMA((8,))]


def body(
    sizes,
    latent,
    control,
    first_mean,
    first_scale,
    first_gain,
    first_shift,
    first_kernel,
    first_bias,
    branch_mean,
    branch_scale,
    branch_gain,
    branch_shift,
    branch_kernel,
    branch_bias,
    proj_weight,
    proj_bias,
    second_mean,
    second_scale,
    second_gain,
    second_shift,
    second_kernel,
    second_bias,
):
    hbm = pl.BlockSpec(memory_space=pl.ANY)
    vmem = pl.BlockSpec(memory_space=pltpu.VMEM)
    return pl.pallas_call(
        functools.partial(kernel, sizes),
        out_shape=jax.ShapeDtypeStruct((BROWS, BCOLS, C), BF16),
        in_specs=[hbm] * 6 + [vmem] * 16,
        out_specs=vmem,
        scratch_shapes=[
            pltpu.VMEM((16, C), F32),
            pltpu.VMEM((BROWS, BCOLS, C), BF16),
            pltpu.VMEM((2, CROWS, C, CCOLS), BF16),
            pltpu.VMEM((4, 3, 3, 256, 256), BF16),
            pltpu.VMEM((4, 3, 4, 64, 256), BF16),
            pltpu.VMEM((4, 1024, 256), BF16),
            pltpu.VMEM((4, 3, 3, C, 64), BF16),
            pltpu.VMEM((2, C, C), BF16),
            pltpu.VMEM((6, CROWS + 1, STRIDE, 128), F32),
            pltpu.VMEM((3, BROWS // 4 + 1, STRIDE, 128), F32),
            pltpu.VMEM((2, CROWS + 2, CCOLS, 1024), BF16),
            pltpu.VMEM((BROWS + 2, BCOLS, 1024), BF16),
            pltpu.VMEM((BROWS + 2, BCOLS, 1024), BF16),
            pltpu.VMEM((2, CROWS + 2, CCOLS, 256), F32),
            pltpu.VMEM((BROWS, BCOLS, C), F32),
            pltpu.VMEM((4, 4, 320, 128), BF16),
            pltpu.VMEM((16, 320, 128), BF16),
            pltpu.VMEM((2, 3, BROWS // 8, 8, 128), F32),
        ]
        + halo_scratch(6, CROWS, CCOLS)
        + halo_scratch(3, BROWS, BCOLS)
        + halo_scratch(3, BROWS, BCOLS)
        + [
            pltpu.SemaphoreType.DMA((4,)),
            pltpu.SemaphoreType.DMA((4, 3)),
            pltpu.SemaphoreType.DMA((3, 4)),
            pltpu.SemaphoreType.DMA((3, 4)),
        ],
        compiler_params=pltpu.CompilerParams(
            collective_id=0, has_side_effects=True, vmem_limit_bytes=67_000_000
        ),
    )(
        latent,
        jnp.transpose(control, (0, 1, 3, 2)),
        first_kernel,
        branch_kernel,
        second_kernel,
        proj_weight,
        first_mean,
        first_scale,
        first_gain,
        first_shift,
        first_bias,
        branch_mean,
        branch_scale,
        branch_gain,
        branch_shift,
        branch_bias,
        proj_bias,
        second_mean,
        second_scale,
        second_gain,
        second_shift,
        second_bias,
    )


def solution(mesh):
    sizes = (mesh.shape["group"], mesh.shape["col"], mesh.shape["row"])
    in_specs = (
        P("group", ("col", "row"), None),
        P(None, ("group", "row"), "col", None),
    ) + (P(),) * 20
    out_specs = P("group", ("col", "row"), None)
    return jax.shard_map(
        functools.partial(body, sizes),
        mesh=mesh,
        in_specs=in_specs,
        out_specs=out_specs,
        check_vma=False,
    )
```

```python
import functools

import jax
import jax.numpy as jnp
from jax import lax
from jax.experimental import pallas as pl
from jax.experimental.pallas import tpu as pltpu
from jax.sharding import PartitionSpec as P

MESH = pl.DeviceIdType.MESH
F32 = jnp.float32
BF16 = jnp.bfloat16
DIRS = [(i, j) for i in (-1, 0, 1) for j in (-1, 0, 1) if (i, j) != (0, 0)]
C = 320
FIRST, BRANCH, SECOND, BIAS = 0, 2, 6, 8
CROWS, CCOLS = 16, 128
BROWS, BCOLS = 64, 32
BLOCK, STRIDE = 128, 144
PART = 4
VMEM_LIMIT = 57 * 2**20
CHUNK = 16


def swish(value, table, at):
    half = value * table[at : at + 1, :] + table[at + 1 : at + 2, :]
    return half + half * jnp.tanh(half)


def widen(stat):
    groups = stat.shape[1]
    across = lax.broadcasted_iota(jnp.int32, (groups, groups), 0)
    along = lax.broadcasted_iota(jnp.int32, (groups, groups), 1)
    column = jnp.sum(
        jnp.where(across == along, jnp.broadcast_to(stat, (groups, groups)), 0.0),
        axis=1,
        keepdims=True,
    )
    first = lax.broadcasted_iota(jnp.int32, (groups, C), 0) * (C // groups)
    channel = lax.broadcasted_iota(jnp.int32, (groups, C), 1)
    inside = (channel >= first) & (channel < first + C // groups)
    return jnp.sum(
        jnp.where(inside, jnp.broadcast_to(column, (groups, C)), 0.0), axis=0, keepdims=True
    )


class Tiling:
    def __init__(self, mesh_sizes, kind):
        g, c, r = (lax.axis_index(a) for a in ("group", "col", "row"))
        ng, nc, nr = mesh_sizes
        self.nr = nr
        self.kind = kind
        if kind == "branch":
            self.row, self.col, self.rows, self.cols = g * nr + r, c, ng * nr, nc
        else:
            self.row, self.col, self.rows, self.cols = g, c * nr + r, ng, nc * nr

    def at(self, i, j):
        row, col = self.row + i, self.col + j
        if self.kind == "branch":
            return (row // self.nr, col, lax.rem(row, self.nr))
        return (row, col // self.nr, lax.rem(col, self.nr))

    def has(self, i, j):
        row, col = self.row + i, self.col + j
        return (row >= 0) & (row < self.rows) & (col >= 0) & (col < self.cols)


class Halo:
    def __init__(self, tiling, image, rows, cols, bufs, raw=None):
        self.raw = raw
        self.tiling, self.image, self.rows, self.cols = tiling, image, rows, cols
        self.srow, self.scol, self.scor, self.rrow, self.rcol, self.rcor, self.ss, self.rs = bufs
        self.planes = image.shape[0]
        self.per = BLOCK // cols
        self.blocks = rows // self.per
        self.flat = image.reshape(self.planes, image.shape[1] * STRIDE, 128)

    def slot(self, i, j, bufs):
        row, col, cor = bufs
        if j == 0:
            return row.at[(i + 1) // 2]
        if i == 0:
            return col.at[(j + 1) // 2]
        return cor.at[(i + 1) + (j + 1) // 2]

    def copy(self, i, j):
        n = DIRS.index((i, j))
        if self.raw is not None and j == 0:
            source = self.raw[0].at[:, 0 if i == -1 else self.rows - 1]
        else:
            source = self.slot(i, j, (self.srow, self.scol, self.scor))
        return pltpu.make_async_remote_copy(
            src_ref=source,
            dst_ref=self.slot(i, j, (self.rrow, self.rcol, self.rcor)),
            send_sem=self.ss.at[n],
            recv_sem=self.rs.at[n],
            device_id=self.tiling.at(i, j),
            device_id_type=MESH,
        )

    def clear(self):
        for i, j in DIRS:
            if self.raw is not None and j == 0:
                continue

            @pl.when(jnp.logical_not(self.tiling.has(-i, -j)))
            def _():
                slot = self.slot(i, j, (self.rrow, self.rcol, self.rcor))
                slot[...] = jnp.zeros(slot.shape, slot.dtype)

    def start(self, dirs):
        for i, j in dirs:

            @pl.when(self.tiling.has(i, j))
            def _():
                self.copy(i, j).start()

    def send(self):
        cols, blocks = self.cols, self.blocks
        edge = {-1: (0, 8), 1: (blocks - 1, 8 + BLOCK - cols)}
        for p in range(self.planes):
            for i in (-1, 1):
                block, at = edge[i]
                if self.raw is None:
                    self.srow[(i + 1) // 2, p] = self.image[
                        p, block, at : at + cols, :
                    ].astype(BF16)
                for j in (-1, 1):
                    pixel = at + (cols - 1) * ((j + 1) // 2)
                    self.scor[(i + 1) + (j + 1) // 2, p] = jnp.broadcast_to(
                        self.image[p, block, pixel : pixel + 1, :], (16, 128)
                    ).astype(BF16)
            for j in (-1, 1):
                for inner in range(self.per):
                    start = 8 + inner * cols + (cols - 1) * ((j + 1) // 2)
                    self.scol[(j + 1) // 2, p, inner * blocks : (inner + 1) * blocks] = self.flat[
                        p, pl.ds(start, blocks, stride=STRIDE), :
                    ].astype(BF16)
        self.start([(i, j) for i, j in DIRS if self.raw is None or j != 0])

    def receive(self, targets, sides):
        cols, blocks = self.cols, self.blocks
        for i, j in DIRS:

            @pl.when(self.tiling.has(-i, -j))
            def _():
                self.copy(i, j).wait_recv()

        for n, target in enumerate(targets):
            for i in (-1, 1):
                if self.raw is not None:
                    here = self.tiling.has(-i, 0)

                    @pl.when(here)
                    def _():
                        place(self.image, 3 * n, blocks, self.raw[1](self.rrow[(i + 1) // 2, n], n))

                    @pl.when(jnp.logical_not(here))
                    def _():
                        place(self.image, 3 * n, blocks, jnp.zeros((BLOCK, C), F32))

                for t in range(3):
                    p = 3 * n + t
                    if self.raw is None:
                        self.image[p, blocks, 8 : 8 + cols, :] = self.rrow[
                            (i + 1) // 2, p
                        ].astype(F32)
                    for j, at in ((1, 7), (-1, 8 + cols)):
                        self.image[p, blocks, at : at + 1, :] = self.rcor[
                            (i + 1) + (j + 1) // 2, p
                        ].astype(F32)[0:1]
                row = 0 if i == 1 else self.rows + 1
                spread(self.image, 3 * n, blocks, cols, target.at[pl.ds(row, 1)])
            for j in (-1, 1):
                for t in range(3):
                    sides[(j + 1) // 2, t, 0 : self.rows // 8] = (
                        self.rcol[(j + 1) // 2, 3 * n + t]
                        .astype(F32)
                        .reshape(self.rows // 8, 8, 128)
                    )
            sub = lax.broadcasted_iota(jnp.int32, (16, 128), 0)
            lane = lax.broadcasted_iota(jnp.int32, (16, 128), 1)
            places = (
                (1, 0, 0, False),
                (1, 1, 128, False),
                (1, 2, 768, True),
                (0, 0, 512, False),
                (0, 1, 640, False),
                (0, 2, 896, True),
            )

            def fix(group, _):
                for s in range(8):
                    k = group * 8 + s
                    row = lax.rem(k, blocks) * self.per + k // blocks + 1
                    for side, t, lanes, leftover in places:
                        edge = (sub == 0) if side == 1 else (sub == 15)
                        if leftover:
                            edge = edge & (lane < 64)
                        at = 0 if side == 1 else cols - 16
                        pixel = jnp.broadcast_to(sides[side, t, group, s : s + 1, :], (16, 128))
                        held = target[row, at : at + 16, lanes : lanes + 128]
                        target[row, at : at + 16, lanes : lanes + 128] = jnp.where(
                            edge, pixel, held.astype(F32)
                        ).astype(BF16)
                return 0

            lax.fori_loop(0, self.rows // 8, fix, 0)

    def finish(self):
        for i, j in DIRS:

            @pl.when(self.tiling.has(i, j))
            def _():
                self.copy(i, j).wait_send()


def place(image, plane, block, value):
    image[plane, block, 8 : 8 + BLOCK, :] = value[:, 0:128]
    image[plane + 1, block, 8 : 8 + BLOCK, :] = value[:, 128:256]
    image[plane + 2, block, 8 : 8 + BLOCK, 0:64] = value[:, 256:320]


def spread(image, plane, block, cols, target):
    rows = target.shape[0]
    size = rows * cols
    rest = []
    for n, start in enumerate((7, 8, 9)):
        for t in range(2):
            piece = image[plane + t, block, start : start + size, :].astype(BF16)
            lanes = n * 256 + t * 128
            target[:, :, lanes : lanes + 128] = piece.reshape(rows, cols, 128)
        rest.append(image[plane + 2, block, start : start + size, :][:, 0:64])
    for lanes, pair in ((768, rest[0:2]), (896, [rest[2], jnp.zeros((size, 64), F32)])):
        piece = jnp.concatenate(pair, axis=1).astype(BF16)
        target[:, :, lanes : lanes + 128] = piece.reshape(rows, cols, 128)


def kernel(
    sizes,
    latent_hbm,
    control_hbm,
    first_hbm,
    branch_hbm,
    second_hbm,
    proj_hbm,
    first_mean,
    first_scale,
    first_gain,
    first_shift,
    first_bias,
    branch_mean,
    branch_scale,
    branch_gain,
    branch_shift,
    branch_bias,
    proj_bias,
    second_mean,
    second_scale,
    second_gain,
    second_shift,
    second_bias,
    outer_hbm,
    got,
    table,
    latent,
    control,
    all_w,
    rest_w,
    proj_w,
    cimage,
    bimage,
    cspread,
    bspread,
    hspread,
    crest,
    outer,
    send,
    sides,
    *more,
):
    halo_bufs = [more[0:8], more[8:16], more[16:24]]
    load_sem, weight_sem, res_send, res_recv, own_sem, outer_sem = more[24:]
    g, c, r = (lax.axis_index(a) for a in ("group", "col", "row"))
    nr = sizes[2]
    ctile, btile = Tiling(sizes, "branch"), Tiling(sizes, "base")

    control_loads = [
        pltpu.make_async_copy(control_hbm.at[k], control.at[k], load_sem.at[k]) for k in range(2)
    ]
    for load in control_loads:
        load.start()

    barrier = pltpu.get_barrier_semaphore()
    count = nr - 1
    for tile in (ctile, btile):
        for i, j in DIRS:
            there = tile.has(i, j)
            count = count + there.astype(jnp.int32)

            @pl.when(there)
            def _():
                pl.semaphore_signal(
                    barrier, inc=1, device_id=tile.at(i, j), device_id_type=MESH
                )

    def peer(step):
        far = lax.rem(r // 2 + 1, 2) * 2
        core = lax.rem(r, 2)
        return (far + core, far + 1 - core, (r // 2) * 2 + 1 - core)[step]

    for step in range(3):
        pl.semaphore_signal(barrier, inc=1, device_id=(g, c, peer(step)), device_id_type=MESH)

    def act_control(value, branch):
        return swish(value.T.astype(F32), table, BRANCH + 2 * branch)

    chalo = Halo(ctile, cimage, CROWS, CCOLS, halo_bufs[0], raw=(control, act_control))
    bhalo = Halo(btile, bimage, BROWS, BCOLS, halo_bufs[1])
    hhalo = Halo(btile, bimage, BROWS, BCOLS, halo_bufs[2])

    norms = ((first_mean, first_scale, first_gain, first_shift, 0),) + tuple(
        (branch_mean, branch_scale, branch_gain, branch_shift, k) for k in range(2)
    ) + ((second_mean, second_scale, second_gain, second_shift, 0),)

    def vector(ref, k):
        return ref[...].reshape(1, -1) if len(ref.shape) == 1 else ref[k : k + 1, :]

    for n, (*stats, k) in enumerate(norms):
        mean, scale, gain, shift = (vector(ref, k) for ref in stats)
        slope = 0.5 * (widen(scale) * gain)
        table[2 * n : 2 * n + 1, :] = slope
        table[2 * n + 1 : 2 * n + 2, :] = 0.5 * shift - widen(mean) * slope
    table[BIAS : BIAS + 2, :] = branch_bias[...]
    table[BIAS + 2 : BIAS + 3, :] = proj_bias[0:1, :] + proj_bias[1:2, :]
    table[BIAS + 3 : BIAS + 4, :] = vector(first_bias, 0)
    table[BIAS + 4 : BIAS + 5, :] = vector(second_bias, 0)

    for load in control_loads:
        load.wait()
    latent_load = pltpu.make_async_copy(latent_hbm, latent, load_sem.at[2])
    proj_load = pltpu.make_async_copy(proj_hbm, proj_w, load_sem.at[3])

    def weight_loads(n):
        ref = (branch_hbm.at[0], branch_hbm.at[1], first_hbm, second_hbm)[n]
        return (pltpu.make_async_copy(ref, all_w.at[n], weight_sem.at[n]),)

    for load in (
        latent_load,
        *weight_loads(0),
        *weight_loads(1),
        proj_load,
        *weight_loads(2),
        *weight_loads(3),
    ):
        load.start()

    pl.semaphore_wait(barrier, count)
    chalo.start([(-1, 0), (1, 0)])
    for branch in range(2):

        def control_rows(n, _):
            for row in (2 * n, 2 * n + 1):
                value = act_control(control[branch, row], branch)
                place(cimage, 3 * branch, row, value)
                spread(cimage, 3 * branch, row, CCOLS, cspread.at[branch, pl.ds(row + 1, 1)])
            return 0

        lax.fori_loop(0, CROWS // 2, control_rows, 0)
    chalo.send()
    chalo.clear()
    bhalo.clear()
    hhalo.clear()

    def arrange(n):
        for load in weight_loads(n):
            load.wait()

        def tap_column(dx, _):
            for at, start, size in ((dx * 256, 0, 256), (768 + dx * 64, 256, 64)):
                pieces = [all_w[n, dy, dx, start : start + size, 256:320] for dy in range(3)]
                rest_w[n, pl.ds(at, size), :] = jnp.concatenate(
                    pieces + [jnp.zeros((size, 64), BF16)], axis=1
                )
            return 0

        lax.fori_loop(0, 3, tap_column, 0)
        rest_w[n, 960:1024, :] = jnp.zeros((64, 256), BF16)

    def main_dot(image_rows, n):
        weight = []
        for dy in range(3):
            weight += [all_w[n, dy, dx, 0:256, 0:256] for dx in range(3)]
            weight += [all_w[n, dy, dx, 256:320, 0:256] for dx in range(3)]
            weight.append(jnp.zeros((64, 256), BF16))
        return jnp.dot(
            jnp.concatenate(image_rows, axis=1),
            jnp.concatenate(weight, axis=0),
            preferred_element_type=F32,
        )

    def act_latent(n):
        value = swish(
            latent[pl.ds(n * 4, 4)].astype(F32).reshape(BLOCK, C), table, FIRST
        )
        place(bimage, 0, n, value)
        spread(bimage, 0, n, BCOLS, bspread.at[pl.ds(n * 4 + 1, 4)])

    def res_copy(step, part):
        q = peer(step)
        return pltpu.make_async_remote_copy(
            src_ref=send.at[q, part],
            dst_ref=got.at[r * 4 + part],
            send_sem=res_send.at[step, part],
            recv_sem=res_recv.at[step, part],
            device_id=(g, c, q),
            device_id_type=MESH,
        )

    def own_copy(part):
        return pltpu.make_async_copy(send.at[r, part], got.at[r * 4 + part], own_sem.at[part])

    def branch_part(part):
        row = part * PART
        first, last = (0, PART + 2) if part == 0 else (row + 2, row + PART + 2)
        features = []
        for branch in range(2):
            size = (last - first) * CCOLS
            crest[branch, first:last] = jnp.dot(
                cspread[branch, first:last].reshape(size, 1024),
                rest_w[branch],
                preferred_element_type=F32,
            ).reshape(last - first, CCOLS, 256)
            main = main_dot(
                [
                    cspread[branch, row + dy : row + dy + PART].reshape(PART * CCOLS, 1024)
                    for dy in range(3)
                ],
                branch,
            )
            rest = (
                crest[branch, row : row + PART, :, 0:64]
                + crest[branch, row + 1 : row + 1 + PART, :, 64:128]
                + crest[branch, row + 2 : row + 2 + PART, :, 128:192]
            ).reshape(PART * CCOLS, 64)
            bias = table[BIAS + branch : BIAS + branch + 1, :]
            features.append(
                ((main + bias[:, 0:256]).astype(BF16), (rest + bias[:, 256:320]).astype(BF16))
            )
        (m0, r0), (m1, r1) = features
        both = jnp.concatenate([m0, m1, jnp.concatenate([r0, r1], axis=1)], axis=1)
        proj = jnp.concatenate(
            [
                proj_w[0, 0:256, :],
                proj_w[1, 0:256, :],
                proj_w[0, 256:320, :],
                proj_w[1, 256:320, :],
            ],
            axis=0,
        )
        residual = jnp.dot(both, proj, preferred_element_type=F32) + table[BIAS + 2 : BIAS + 3, :]
        residual = residual.reshape(PART, CCOLS, C)
        for q in range(4):
            block = residual[:, q * BCOLS : (q + 1) * BCOLS, :].reshape(BLOCK, C)
            send[q, part, 0:128] = block[:, 0:128].astype(BF16)
            send[q, part, 128:256] = block[:, 128:256].astype(BF16)
            send[q, part, 256:320] = jnp.concatenate(
                [block[0:64, 256:320], block[64:128, 256:320]], axis=1
            ).astype(BF16)
        for step in range(3):
            res_copy(step, part).start()
        own_copy(part).start()

    def conv_base(n, image, row, bias_at):
        main = main_dot(
            [image[row + dy : row + dy + CHUNK].reshape(CHUNK * BCOLS, 1024) for dy in range(3)],
            n,
        )
        every = jnp.dot(
            image[row : row + CHUNK + 2].reshape((CHUNK + 2) * BCOLS, 1024),
            rest_w[n],
            preferred_element_type=F32,
        )
        size = CHUNK * BCOLS
        rest = (
            every[0:size, 0:64]
            + every[BCOLS : BCOLS + size, 64:128]
            + every[2 * BCOLS : 2 * BCOLS + size, 128:192]
        )
        bias = table[bias_at : bias_at + 1, :]
        return jnp.concatenate([main + bias[:, 0:256], rest + bias[:, 256:320]], axis=1)

    latent_load.wait()

    def latent_blocks(n, _):
        act_latent(2 * n)
        act_latent(2 * n + 1)
        return 0

    lax.fori_loop(0, BROWS // 8, latent_blocks, 0)
    bhalo.send()
    arrange(0)
    arrange(1)
    proj_load.wait()
    chalo.receive([cspread.at[0], cspread.at[1]], sides)
    branch_part(0)
    branch_part(1)
    arrange(2)

    bhalo.receive([bspread], sides)
    for row in range(0, BROWS, CHUNK):
        value = swish(conv_base(2, bspread, row, BIAS + 3), table, SECOND)
        for k in range(CHUNK // 4):
            place(bimage, 0, row // 4 + k, value[k * BLOCK : (k + 1) * BLOCK])
            spread(
                bimage, 0, row // 4 + k, BCOLS, hspread.at[pl.ds(row + 4 * k + 1, 4)]
            )
    hhalo.send()

    branch_part(2)
    branch_part(3)
    arrange(3)

    hhalo.receive([hspread], sides)

    def outer_copy(row):
        rows = pl.ds(row, CHUNK)
        return pltpu.make_async_copy(
            outer.at[rows], outer_hbm.at[rows], outer_sem.at[row // CHUNK]
        )

    for row in range(0, BROWS, CHUNK):
        value = conv_base(3, hspread, row, BIAS + 4).reshape(CHUNK, BCOLS, C)
        outer[row : row + CHUNK] = value + latent[row : row + CHUNK].astype(F32)
        outer_copy(row).start()

    for part in range(4):
        own_copy(part).wait()
        for step in range(3):
            res_copy(step, part).wait()
    for row in range(0, BROWS, CHUNK):
        outer_copy(row).wait()
    for halo in (chalo, bhalo, hhalo):
        halo.finish()


def add_residual(outer, got, out):
    for n in range(CHUNK // 4):
        rows = slice(4 * n, 4 * n + 4)
        rest = got[n, 256:320]
        pieces = (
            got[n, 0:128],
            got[n, 128:256],
            jnp.concatenate([rest[:, 0:64], rest[:, 64:128]], axis=0),
        )
        for lanes, piece in zip((slice(0, 128), slice(128, 256), slice(256, 320)), pieces):
            total = outer[rows, :, lanes].reshape(BLOCK, -1) + piece.astype(F32)
            out[rows, :, lanes] = total.astype(BF16).reshape(4, BCOLS, -1)


def halo_scratch(planes, rows, cols, raw=False):
    row = pltpu.VMEM((2, 2, C, 128) if raw else (2, planes, cols, 128), BF16)
    both = [
        row,
        pltpu.VMEM((2, planes, rows, 128), BF16),
        pltpu.VMEM((4, planes, 16, 128), BF16),
    ]
    send = [pltpu.VMEM((8, 128), BF16)] + both[1:] if raw else both
    return send + both + [pltpu.SemaphoreType.DMA((8,)), pltpu.SemaphoreType.DMA((8,))]


def body(
    sizes,
    latent,
    control,
    first_mean,
    first_scale,
    first_gain,
    first_shift,
    first_kernel,
    first_bias,
    branch_mean,
    branch_scale,
    branch_gain,
    branch_shift,
    branch_kernel,
    branch_bias,
    proj_weight,
    proj_bias,
    second_mean,
    second_scale,
    second_gain,
    second_shift,
    second_kernel,
    second_bias,
):
    hbm = pl.BlockSpec(memory_space=pl.ANY)
    vmem = pl.BlockSpec(memory_space=pltpu.VMEM)
    outer, residual = pl.pallas_call(
        functools.partial(kernel, sizes),
        out_shape=(
            jax.ShapeDtypeStruct((BROWS, BCOLS, C), F32),
            jax.ShapeDtypeStruct((16, 320, 128), BF16),
        ),
        in_specs=[hbm] * 6 + [vmem] * 16,
        out_specs=(hbm, hbm),
        scratch_shapes=[
            pltpu.VMEM((16, C), F32),
            pltpu.VMEM((BROWS, BCOLS, C), BF16),
            pltpu.VMEM((2, CROWS, C, CCOLS), BF16),
            pltpu.VMEM((4, 3, 3, C, C), BF16),
            pltpu.VMEM((4, 1024, 256), BF16),
            pltpu.VMEM((2, C, C), BF16),
            pltpu.VMEM((6, CROWS + 1, STRIDE, 128), F32),
            pltpu.VMEM((3, BROWS // 4 + 1, STRIDE, 128), F32),
            pltpu.VMEM((2, CROWS + 2, CCOLS, 1024), BF16),
            pltpu.VMEM((BROWS + 2, BCOLS, 1024), BF16),
            pltpu.VMEM((BROWS + 2, BCOLS, 1024), BF16),
            pltpu.VMEM((2, CROWS + 2, CCOLS, 256), F32),
            pltpu.VMEM((BROWS, BCOLS, C), F32),
            pltpu.VMEM((4, 4, 320, 128), BF16),
            pltpu.VMEM((2, 3, BROWS // 8, 8, 128), F32),
        ]
        + halo_scratch(6, CROWS, CCOLS, raw=True)
        + halo_scratch(3, BROWS, BCOLS)
        + halo_scratch(3, BROWS, BCOLS)
        + [
            pltpu.SemaphoreType.DMA((4,)),
            pltpu.SemaphoreType.DMA((4,)),
            pltpu.SemaphoreType.DMA((3, 4)),
            pltpu.SemaphoreType.DMA((3, 4)),
            pltpu.SemaphoreType.DMA((4,)),
            pltpu.SemaphoreType.DMA((4,)),
        ],
        compiler_params=pltpu.CompilerParams(
            collective_id=0, has_side_effects=True, vmem_limit_bytes=VMEM_LIMIT
        ),
    )(
        latent,
        jnp.transpose(control, (0, 1, 3, 2)),
        first_kernel,
        branch_kernel,
        second_kernel,
        proj_weight,
        first_mean,
        first_scale,
        first_gain,
        first_shift,
        first_bias,
        branch_mean,
        branch_scale,
        branch_gain,
        branch_shift,
        branch_bias,
        proj_bias,
        second_mean,
        second_scale,
        second_gain,
        second_shift,
        second_bias,
    )
    rows = pl.BlockSpec((CHUNK, BCOLS, C), lambda n: (n, 0, 0))
    return pl.pallas_call(
        add_residual,
        grid=(BROWS // CHUNK,),
        out_shape=jax.ShapeDtypeStruct((BROWS, BCOLS, C), BF16),
        in_specs=[rows, pl.BlockSpec((4, 320, 128), lambda n: (n, 0, 0))],
        out_specs=rows,
    )(outer, residual)


def solution(mesh):
    sizes = (mesh.shape["group"], mesh.shape["col"], mesh.shape["row"])
    in_specs = (
        P("group", ("col", "row"), None),
        P(None, ("group", "row"), "col", None),
    ) + (P(),) * 20
    out_specs = P("group", ("col", "row"), None)
    return jax.shard_map(
        functools.partial(body, sizes),
        mesh=mesh,
        in_specs=in_specs,
        out_specs=out_specs,
        check_vma=False,
    )
```

```python
import functools

import jax
import jax.numpy as jnp
from jax import lax
from jax.experimental import pallas as pl
from jax.experimental.pallas import tpu as pltpu
from jax.sharding import PartitionSpec as P

MESH = pl.DeviceIdType.MESH
F32 = jnp.float32
BF16 = jnp.bfloat16
DIRS = [(i, j) for i in (-1, 0, 1) for j in (-1, 0, 1) if (i, j) != (0, 0)]
C = 320
FIRST, BRANCH, SECOND, BIAS = 0, 2, 6, 8
CROWS, CCOLS = 16, 128
BROWS, BCOLS = 64, 32
BLOCK, STRIDE = 128, 144
PART = 4
VMEM_LIMIT = 56 * 2**20
CHUNK = 16


def swish(value, table, at):
    half = value * table[at : at + 1, :] + table[at + 1 : at + 2, :]
    return half + half * jnp.tanh(half)


def widen(stat):
    groups = stat.shape[1]
    across = lax.broadcasted_iota(jnp.int32, (groups, groups), 0)
    along = lax.broadcasted_iota(jnp.int32, (groups, groups), 1)
    column = jnp.sum(
        jnp.where(across == along, jnp.broadcast_to(stat, (groups, groups)), 0.0),
        axis=1,
        keepdims=True,
    )
    first = lax.broadcasted_iota(jnp.int32, (groups, C), 0) * (C // groups)
    channel = lax.broadcasted_iota(jnp.int32, (groups, C), 1)
    inside = (channel >= first) & (channel < first + C // groups)
    return jnp.sum(
        jnp.where(inside, jnp.broadcast_to(column, (groups, C)), 0.0), axis=0, keepdims=True
    )


class Tiling:
    def __init__(self, mesh_sizes, kind):
        g, c, r = (lax.axis_index(a) for a in ("group", "col", "row"))
        ng, nc, nr = mesh_sizes
        self.nr = nr
        self.kind = kind
        if kind == "branch":
            self.row, self.col, self.rows, self.cols = g * nr + r, c, ng * nr, nc
        else:
            self.row, self.col, self.rows, self.cols = g, c * nr + r, ng, nc * nr

    def at(self, i, j):
        row, col = self.row + i, self.col + j
        if self.kind == "branch":
            return (row // self.nr, col, lax.rem(row, self.nr))
        return (row, col // self.nr, lax.rem(col, self.nr))

    def has(self, i, j):
        row, col = self.row + i, self.col + j
        return (row >= 0) & (row < self.rows) & (col >= 0) & (col < self.cols)


class Halo:
    def __init__(self, tiling, image, rows, cols, bufs, raw=None):
        self.raw = raw
        self.tiling, self.image, self.rows, self.cols = tiling, image, rows, cols
        self.srow, self.scol, self.scor, self.rrow, self.rcol, self.rcor, self.ss, self.rs = bufs
        self.planes = image.shape[0]
        self.per = BLOCK // cols
        self.blocks = rows // self.per
        self.flat = image.reshape(self.planes, image.shape[1] * STRIDE, 128)

    def slot(self, i, j, bufs):
        row, col, cor = bufs
        if j == 0:
            return row.at[(i + 1) // 2]
        if i == 0:
            return col.at[(j + 1) // 2]
        return cor.at[(i + 1) + (j + 1) // 2]

    def copy(self, i, j):
        n = DIRS.index((i, j))
        if self.raw is not None and j == 0:
            source = self.raw[0].at[:, 0 if i == -1 else self.rows - 1]
        else:
            source = self.slot(i, j, (self.srow, self.scol, self.scor))
        return pltpu.make_async_remote_copy(
            src_ref=source,
            dst_ref=self.slot(i, j, (self.rrow, self.rcol, self.rcor)),
            send_sem=self.ss.at[n],
            recv_sem=self.rs.at[n],
            device_id=self.tiling.at(i, j),
            device_id_type=MESH,
        )

    def clear(self):
        for i, j in DIRS:
            if self.raw is not None and j == 0:
                continue

            @pl.when(jnp.logical_not(self.tiling.has(-i, -j)))
            def _():
                slot = self.slot(i, j, (self.rrow, self.rcol, self.rcor))
                slot[...] = jnp.zeros(slot.shape, slot.dtype)

    def start(self, dirs):
        for i, j in dirs:

            @pl.when(self.tiling.has(i, j))
            def _():
                self.copy(i, j).start()

    def send(self):
        cols, blocks = self.cols, self.blocks
        edge = {-1: (0, 8), 1: (blocks - 1, 8 + BLOCK - cols)}
        for p in range(self.planes):
            for i in (-1, 1):
                block, at = edge[i]
                if self.raw is None:
                    self.srow[(i + 1) // 2, p] = self.image[
                        p, block, at : at + cols, :
                    ].astype(BF16)
                for j in (-1, 1):
                    pixel = at + (cols - 1) * ((j + 1) // 2)
                    self.scor[(i + 1) + (j + 1) // 2, p] = jnp.broadcast_to(
                        self.image[p, block, pixel : pixel + 1, :], (16, 128)
                    ).astype(BF16)
            for j in (-1, 1):
                for inner in range(self.per):
                    start = 8 + inner * cols + (cols - 1) * ((j + 1) // 2)
                    self.scol[(j + 1) // 2, p, inner * blocks : (inner + 1) * blocks] = self.flat[
                        p, pl.ds(start, blocks, stride=STRIDE), :
                    ].astype(BF16)
        self.start([(i, j) for i, j in DIRS if self.raw is None or j != 0])

    def receive(self, targets, sides):
        cols, blocks = self.cols, self.blocks
        for i, j in DIRS:

            @pl.when(self.tiling.has(-i, -j))
            def _():
                self.copy(i, j).wait_recv()

        for n, target in enumerate(targets):
            for i in (-1, 1):
                if self.raw is not None:
                    here = self.tiling.has(-i, 0)

                    @pl.when(here)
                    def _():
                        place(self.image, 3 * n, blocks, self.raw[1](self.rrow[(i + 1) // 2, n], n))

                    @pl.when(jnp.logical_not(here))
                    def _():
                        place(self.image, 3 * n, blocks, jnp.zeros((BLOCK, C), F32))

                for t in range(3):
                    p = 3 * n + t
                    if self.raw is None:
                        self.image[p, blocks, 8 : 8 + cols, :] = self.rrow[
                            (i + 1) // 2, p
                        ].astype(F32)
                    for j, at in ((1, 7), (-1, 8 + cols)):
                        self.image[p, blocks, at : at + 1, :] = self.rcor[
                            (i + 1) + (j + 1) // 2, p
                        ].astype(F32)[0:1]
                row = 0 if i == 1 else self.rows + 1
                spread(self.image, 3 * n, blocks, cols, target.at[pl.ds(row, 1)])
            for j in (-1, 1):
                for t in range(3):
                    sides[(j + 1) // 2, t, 0 : self.rows // 8] = (
                        self.rcol[(j + 1) // 2, 3 * n + t]
                        .astype(F32)
                        .reshape(self.rows // 8, 8, 128)
                    )
            sub = lax.broadcasted_iota(jnp.int32, (16, 128), 0)
            lane = lax.broadcasted_iota(jnp.int32, (16, 128), 1)
            places = (
                (1, 0, 0, False),
                (1, 1, 128, False),
                (1, 2, 768, True),
                (0, 0, 512, False),
                (0, 1, 640, False),
                (0, 2, 896, True),
            )

            def fix(group, _):
                for s in range(8):
                    k = group * 8 + s
                    row = lax.rem(k, blocks) * self.per + k // blocks + 1
                    for side, t, lanes, leftover in places:
                        edge = (sub == 0) if side == 1 else (sub == 15)
                        if leftover:
                            edge = edge & (lane < 64)
                        at = 0 if side == 1 else cols - 16
                        pixel = jnp.broadcast_to(sides[side, t, group, s : s + 1, :], (16, 128))
                        held = target[row, at : at + 16, lanes : lanes + 128]
                        target[row, at : at + 16, lanes : lanes + 128] = jnp.where(
                            edge, pixel, held.astype(F32)
                        ).astype(BF16)
                return 0

            lax.fori_loop(0, self.rows // 8, fix, 0)

    def finish(self):
        for i, j in DIRS:

            @pl.when(self.tiling.has(i, j))
            def _():
                self.copy(i, j).wait_send()


def place(image, plane, block, value):
    image[plane, block, 8 : 8 + BLOCK, :] = value[:, 0:128]
    image[plane + 1, block, 8 : 8 + BLOCK, :] = value[:, 128:256]
    image[plane + 2, block, 8 : 8 + BLOCK, 0:64] = value[:, 256:320]


def spread(image, plane, block, cols, target):
    rows = target.shape[0]
    size = rows * cols
    rest = []
    for n, start in enumerate((7, 8, 9)):
        for t in range(2):
            piece = image[plane + t, block, start : start + size, :].astype(BF16)
            lanes = n * 256 + t * 128
            target[:, :, lanes : lanes + 128] = piece.reshape(rows, cols, 128)
        rest.append(image[plane + 2, block, start : start + size, :][:, 0:64])
    for lanes, pair in ((768, rest[0:2]), (896, [rest[2], jnp.zeros((size, 64), F32)])):
        piece = jnp.concatenate(pair, axis=1).astype(BF16)
        target[:, :, lanes : lanes + 128] = piece.reshape(rows, cols, 128)


def kernel(
    sizes,
    latent_hbm,
    control_hbm,
    first_hbm,
    branch_hbm,
    second_hbm,
    proj_hbm,
    first_mean,
    first_scale,
    first_gain,
    first_shift,
    first_bias,
    branch_mean,
    branch_scale,
    branch_gain,
    branch_shift,
    branch_bias,
    proj_bias,
    second_mean,
    second_scale,
    second_gain,
    second_shift,
    second_bias,
    outer,
    got,
    table,
    latent,
    control,
    all_w,
    rest_w,
    proj_w,
    cimage,
    bimage,
    cspread,
    bspread,
    hspread,
    crest,
    send,
    sides,
    *more,
):
    halo_bufs = [more[0:8], more[8:16], more[16:24]]
    load_sem, weight_sem, res_send, res_recv, own_sem = more[24:]
    g, c, r = (lax.axis_index(a) for a in ("group", "col", "row"))
    nr = sizes[2]
    ctile, btile = Tiling(sizes, "branch"), Tiling(sizes, "base")

    control_loads = [
        pltpu.make_async_copy(control_hbm.at[k], control.at[k], load_sem.at[k]) for k in range(2)
    ]
    for load in control_loads:
        load.start()

    barrier = pltpu.get_barrier_semaphore()
    count = nr - 1
    for tile in (ctile, btile):
        for i, j in DIRS:
            there = tile.has(i, j)
            count = count + there.astype(jnp.int32)

            @pl.when(there)
            def _():
                pl.semaphore_signal(
                    barrier, inc=1, device_id=tile.at(i, j), device_id_type=MESH
                )

    def peer(step):
        far = lax.rem(r // 2 + 1, 2) * 2
        core = lax.rem(r, 2)
        return (far + core, far + 1 - core, (r // 2) * 2 + 1 - core)[step]

    for step in range(3):
        pl.semaphore_signal(barrier, inc=1, device_id=(g, c, peer(step)), device_id_type=MESH)

    def act_control(value, branch):
        return swish(value.T.astype(F32), table, BRANCH + 2 * branch)

    chalo = Halo(ctile, cimage, CROWS, CCOLS, halo_bufs[0], raw=(control, act_control))
    bhalo = Halo(btile, bimage, BROWS, BCOLS, halo_bufs[1])
    hhalo = Halo(btile, bimage, BROWS, BCOLS, halo_bufs[2])

    norms = ((first_mean, first_scale, first_gain, first_shift, 0),) + tuple(
        (branch_mean, branch_scale, branch_gain, branch_shift, k) for k in range(2)
    ) + ((second_mean, second_scale, second_gain, second_shift, 0),)

    def vector(ref, k):
        return ref[...].reshape(1, -1) if len(ref.shape) == 1 else ref[k : k + 1, :]

    for n, (*stats, k) in enumerate(norms):
        mean, scale, gain, shift = (vector(ref, k) for ref in stats)
        slope = 0.5 * (widen(scale) * gain)
        table[2 * n : 2 * n + 1, :] = slope
        table[2 * n + 1 : 2 * n + 2, :] = 0.5 * shift - widen(mean) * slope
    table[BIAS : BIAS + 2, :] = branch_bias[...]
    table[BIAS + 2 : BIAS + 3, :] = proj_bias[0:1, :] + proj_bias[1:2, :]
    table[BIAS + 3 : BIAS + 4, :] = vector(first_bias, 0)
    table[BIAS + 4 : BIAS + 5, :] = vector(second_bias, 0)

    for load in control_loads:
        load.wait()
    latent_load = pltpu.make_async_copy(latent_hbm, latent, load_sem.at[2])
    proj_load = pltpu.make_async_copy(proj_hbm, proj_w, load_sem.at[3])

    def weight_loads(n):
        ref = (branch_hbm.at[0], branch_hbm.at[1], first_hbm, second_hbm)[n]
        return (pltpu.make_async_copy(ref, all_w.at[n], weight_sem.at[n]),)

    for load in (
        latent_load,
        *weight_loads(0),
        *weight_loads(1),
        proj_load,
        *weight_loads(2),
        *weight_loads(3),
    ):
        load.start()

    pl.semaphore_wait(barrier, count)
    chalo.start([(-1, 0), (1, 0)])
    for branch in range(2):

        def control_rows(n, _):
            for row in (2 * n, 2 * n + 1):
                value = act_control(control[branch, row], branch)
                place(cimage, 3 * branch, row, value)
                spread(cimage, 3 * branch, row, CCOLS, cspread.at[branch, pl.ds(row + 1, 1)])
            return 0

        lax.fori_loop(0, CROWS // 2, control_rows, 0)
    chalo.send()
    chalo.clear()
    bhalo.clear()
    hhalo.clear()

    def arrange(n):
        for load in weight_loads(n):
            load.wait()

        def tap_column(dx, _):
            for at, start, size in ((dx * 256, 0, 256), (768 + dx * 64, 256, 64)):
                pieces = [all_w[n, dy, dx, start : start + size, 256:320] for dy in range(3)]
                rest_w[n, pl.ds(at, size), :] = jnp.concatenate(
                    pieces + [jnp.zeros((size, 64), BF16)], axis=1
                )
            return 0

        lax.fori_loop(0, 3, tap_column, 0)
        rest_w[n, 960:1024, :] = jnp.zeros((64, 256), BF16)

    def main_dot(image_rows, n):
        weight = []
        for dy in range(3):
            weight += [all_w[n, dy, dx, 0:256, 0:256] for dx in range(3)]
            weight += [all_w[n, dy, dx, 256:320, 0:256] for dx in range(3)]
            weight.append(jnp.zeros((64, 256), BF16))
        return jnp.dot(
            jnp.concatenate(image_rows, axis=1),
            jnp.concatenate(weight, axis=0),
            preferred_element_type=F32,
        )

    def act_latent(n):
        value = swish(
            latent[pl.ds(n * 4, 4)].astype(F32).reshape(BLOCK, C), table, FIRST
        )
        place(bimage, 0, n, value)
        spread(bimage, 0, n, BCOLS, bspread.at[pl.ds(n * 4 + 1, 4)])

    def res_copy(step, part):
        q = peer(step)
        return pltpu.make_async_remote_copy(
            src_ref=send.at[q, part],
            dst_ref=got.at[r * 4 + part],
            send_sem=res_send.at[step, part],
            recv_sem=res_recv.at[step, part],
            device_id=(g, c, q),
            device_id_type=MESH,
        )

    def own_copy(part):
        return pltpu.make_async_copy(send.at[r, part], got.at[r * 4 + part], own_sem.at[part])

    def branch_part(part):
        row = part * PART
        first, last = (0, PART + 2) if part == 0 else (row + 2, row + PART + 2)
        features = []
        for branch in range(2):
            size = (last - first) * CCOLS
            crest[branch, first:last] = jnp.dot(
                cspread[branch, first:last].reshape(size, 1024),
                rest_w[branch],
                preferred_element_type=F32,
            ).reshape(last - first, CCOLS, 256)
            main = main_dot(
                [
                    cspread[branch, row + dy : row + dy + PART].reshape(PART * CCOLS, 1024)
                    for dy in range(3)
                ],
                branch,
            )
            rest = (
                crest[branch, row : row + PART, :, 0:64]
                + crest[branch, row + 1 : row + 1 + PART, :, 64:128]
                + crest[branch, row + 2 : row + 2 + PART, :, 128:192]
            ).reshape(PART * CCOLS, 64)
            bias = table[BIAS + branch : BIAS + branch + 1, :]
            features.append(
                ((main + bias[:, 0:256]).astype(BF16), (rest + bias[:, 256:320]).astype(BF16))
            )
        (m0, r0), (m1, r1) = features
        both = jnp.concatenate([m0, m1, jnp.concatenate([r0, r1], axis=1)], axis=1)
        proj = jnp.concatenate(
            [
                proj_w[0, 0:256, :],
                proj_w[1, 0:256, :],
                proj_w[0, 256:320, :],
                proj_w[1, 256:320, :],
            ],
            axis=0,
        )
        residual = jnp.dot(both, proj, preferred_element_type=F32) + table[BIAS + 2 : BIAS + 3, :]
        residual = residual.reshape(PART, CCOLS, C)
        for q in range(4):
            block = residual[:, q * BCOLS : (q + 1) * BCOLS, :].reshape(BLOCK, C)
            send[q, part, 0:128] = block[:, 0:128].astype(BF16)
            send[q, part, 128:256] = block[:, 128:256].astype(BF16)
            send[q, part, 256:320] = jnp.concatenate(
                [block[0:64, 256:320], block[64:128, 256:320]], axis=1
            ).astype(BF16)
        for step in range(3):
            res_copy(step, part).start()
        own_copy(part).start()

    def conv_base(n, image, row, bias_at):
        main = main_dot(
            [image[row + dy : row + dy + CHUNK].reshape(CHUNK * BCOLS, 1024) for dy in range(3)],
            n,
        )
        every = jnp.dot(
            image[row : row + CHUNK + 2].reshape((CHUNK + 2) * BCOLS, 1024),
            rest_w[n],
            preferred_element_type=F32,
        )
        size = CHUNK * BCOLS
        rest = (
            every[0:size, 0:64]
            + every[BCOLS : BCOLS + size, 64:128]
            + every[2 * BCOLS : 2 * BCOLS + size, 128:192]
        )
        bias = table[bias_at : bias_at + 1, :]
        return jnp.concatenate([main + bias[:, 0:256], rest + bias[:, 256:320]], axis=1)

    latent_load.wait()

    def latent_blocks(n, _):
        act_latent(2 * n)
        act_latent(2 * n + 1)
        return 0

    lax.fori_loop(0, BROWS // 8, latent_blocks, 0)
    bhalo.send()
    arrange(0)
    arrange(1)
    proj_load.wait()
    chalo.receive([cspread.at[0], cspread.at[1]], sides)
    branch_part(0)
    branch_part(1)
    arrange(2)

    bhalo.receive([bspread], sides)
    for row in range(0, BROWS, CHUNK):
        value = swish(conv_base(2, bspread, row, BIAS + 3), table, SECOND)
        for k in range(CHUNK // 4):
            place(bimage, 0, row // 4 + k, value[k * BLOCK : (k + 1) * BLOCK])
            spread(
                bimage, 0, row // 4 + k, BCOLS, hspread.at[pl.ds(row + 4 * k + 1, 4)]
            )
    hhalo.send()

    branch_part(2)
    branch_part(3)
    arrange(3)

    hhalo.receive([hspread], sides)
    for row in range(0, BROWS, CHUNK):
        value = conv_base(3, hspread, row, BIAS + 4).reshape(CHUNK, BCOLS, C)
        outer[row : row + CHUNK] = value + latent[row : row + CHUNK].astype(F32)

    for part in range(4):
        own_copy(part).wait()
        for step in range(3):
            res_copy(step, part).wait()
    for halo in (chalo, bhalo, hhalo):
        halo.finish()


def add_residual(outer, got, out_hbm, out, sem):
    def copy(n):
        rows = pl.ds(n * CHUNK, CHUNK)
        return pltpu.make_async_copy(out.at[rows], out_hbm.at[rows], sem.at[n])

    for n in range(BROWS // CHUNK):
        for k in range(n * CHUNK // 4, (n + 1) * CHUNK // 4):
            rows = slice(4 * k, 4 * k + 4)
            rest = got[k, 256:320]
            pieces = (
                got[k, 0:128],
                got[k, 128:256],
                jnp.concatenate([rest[:, 0:64], rest[:, 64:128]], axis=0),
            )
            for lanes, piece in zip((slice(0, 128), slice(128, 256), slice(256, 320)), pieces):
                total = outer[rows, :, lanes].reshape(BLOCK, -1) + piece.astype(F32)
                out[rows, :, lanes] = total.astype(BF16).reshape(4, BCOLS, -1)
        copy(n).start()
    for n in range(BROWS // CHUNK):
        copy(n).wait()


def halo_scratch(planes, rows, cols, raw=False):
    row = pltpu.VMEM((2, 2, C, 128) if raw else (2, planes, cols, 128), BF16)
    both = [
        row,
        pltpu.VMEM((2, planes, rows, 128), BF16),
        pltpu.VMEM((4, planes, 16, 128), BF16),
    ]
    send = [pltpu.VMEM((8, 128), BF16)] + both[1:] if raw else both
    return send + both + [pltpu.SemaphoreType.DMA((8,)), pltpu.SemaphoreType.DMA((8,))]


def body(
    sizes,
    latent,
    control,
    first_mean,
    first_scale,
    first_gain,
    first_shift,
    first_kernel,
    first_bias,
    branch_mean,
    branch_scale,
    branch_gain,
    branch_shift,
    branch_kernel,
    branch_bias,
    proj_weight,
    proj_bias,
    second_mean,
    second_scale,
    second_gain,
    second_shift,
    second_kernel,
    second_bias,
):
    hbm = pl.BlockSpec(memory_space=pl.ANY)
    vmem = pl.BlockSpec(memory_space=pltpu.VMEM)
    outer, residual = pl.pallas_call(
        functools.partial(kernel, sizes),
        out_shape=(
            pltpu.VMEM((BROWS, BCOLS, C), F32),
            pltpu.VMEM((16, 320, 128), BF16),
        ),
        in_specs=[hbm] * 6 + [vmem] * 16,
        out_specs=(vmem, vmem),
        scratch_shapes=[
            pltpu.VMEM((16, C), F32),
            pltpu.VMEM((BROWS, BCOLS, C), BF16),
            pltpu.VMEM((2, CROWS, C, CCOLS), BF16),
            pltpu.VMEM((4, 3, 3, C, C), BF16),
            pltpu.VMEM((4, 1024, 256), BF16),
            pltpu.VMEM((2, C, C), BF16),
            pltpu.VMEM((6, CROWS + 1, STRIDE, 128), F32),
            pltpu.VMEM((3, BROWS // 4 + 1, STRIDE, 128), F32),
            pltpu.VMEM((2, CROWS + 2, CCOLS, 1024), BF16),
            pltpu.VMEM((BROWS + 2, BCOLS, 1024), BF16),
            pltpu.VMEM((BROWS + 2, BCOLS, 1024), BF16),
            pltpu.VMEM((2, CROWS + 2, CCOLS, 256), F32),
            pltpu.VMEM((4, 4, 320, 128), BF16),
            pltpu.VMEM((2, 3, BROWS // 8, 8, 128), F32),
        ]
        + halo_scratch(6, CROWS, CCOLS, raw=True)
        + halo_scratch(3, BROWS, BCOLS)
        + halo_scratch(3, BROWS, BCOLS)
        + [
            pltpu.SemaphoreType.DMA((4,)),
            pltpu.SemaphoreType.DMA((4,)),
            pltpu.SemaphoreType.DMA((3, 4)),
            pltpu.SemaphoreType.DMA((3, 4)),
            pltpu.SemaphoreType.DMA((4,)),
        ],
        compiler_params=pltpu.CompilerParams(
            collective_id=0, has_side_effects=True, vmem_limit_bytes=VMEM_LIMIT
        ),
    )(
        latent,
        jnp.transpose(control, (0, 1, 3, 2)),
        first_kernel,
        branch_kernel,
        second_kernel,
        proj_weight,
        first_mean,
        first_scale,
        first_gain,
        first_shift,
        first_bias,
        branch_mean,
        branch_scale,
        branch_gain,
        branch_shift,
        branch_bias,
        proj_bias,
        second_mean,
        second_scale,
        second_gain,
        second_shift,
        second_bias,
    )
    return pl.pallas_call(
        add_residual,
        out_shape=jax.ShapeDtypeStruct((BROWS, BCOLS, C), BF16),
        in_specs=[vmem, vmem],
        out_specs=hbm,
        scratch_shapes=[
            pltpu.VMEM((BROWS, BCOLS, C), BF16),
            pltpu.SemaphoreType.DMA((BROWS // CHUNK,)),
        ],
        compiler_params=pltpu.CompilerParams(vmem_limit_bytes=16 * 2**20),
    )(outer, residual)


def solution(mesh):
    sizes = (mesh.shape["group"], mesh.shape["col"], mesh.shape["row"])
    in_specs = (
        P("group", ("col", "row"), None),
        P(None, ("group", "row"), "col", None),
    ) + (P(),) * 20
    out_specs = P("group", ("col", "row"), None)
    return jax.shard_map(
        functools.partial(body, sizes),
        mesh=mesh,
        in_specs=in_specs,
        out_specs=out_specs,
        check_vma=False,
    )
```

```python
import functools

import jax
import jax.numpy as jnp
from jax import lax
from jax.experimental import pallas as pl
from jax.experimental.pallas import tpu as pltpu
from jax.sharding import PartitionSpec as P

MESH = pl.DeviceIdType.MESH
F32 = jnp.float32
BF16 = jnp.bfloat16
DIRS = [(i, j) for i in (-1, 0, 1) for j in (-1, 0, 1) if (i, j) != (0, 0)]
C = 320
FIRST, BRANCH, SECOND, BIAS = 0, 2, 6, 8
CROWS, CCOLS = 16, 128
BROWS, BCOLS = 64, 32
BLOCK, STRIDE = 128, 144
PART = 4
VMEM_LIMIT = 56 * 2**20
CHUNK = 16


def swish(value, table, at):
    half = value * table[at : at + 1, :] + table[at + 1 : at + 2, :]
    return half + half * jnp.tanh(half)


def widen(stat):
    groups = stat.shape[1]
    across = lax.broadcasted_iota(jnp.int32, (groups, groups), 0)
    along = lax.broadcasted_iota(jnp.int32, (groups, groups), 1)
    column = jnp.sum(
        jnp.where(across == along, jnp.broadcast_to(stat, (groups, groups)), 0.0),
        axis=1,
        keepdims=True,
    )
    first = lax.broadcasted_iota(jnp.int32, (groups, C), 0) * (C // groups)
    channel = lax.broadcasted_iota(jnp.int32, (groups, C), 1)
    inside = (channel >= first) & (channel < first + C // groups)
    return jnp.sum(
        jnp.where(inside, jnp.broadcast_to(column, (groups, C)), 0.0), axis=0, keepdims=True
    )


class Tiling:
    def __init__(self, mesh_sizes, kind):
        g, c, r = (lax.axis_index(a) for a in ("group", "col", "row"))
        ng, nc, nr = mesh_sizes
        self.nr = nr
        self.kind = kind
        if kind == "branch":
            self.row, self.col, self.rows, self.cols = g * nr + r, c, ng * nr, nc
        else:
            self.row, self.col, self.rows, self.cols = g, c * nr + r, ng, nc * nr

    def at(self, i, j):
        row, col = self.row + i, self.col + j
        if self.kind == "branch":
            return (row // self.nr, col, lax.rem(row, self.nr))
        return (row, col // self.nr, lax.rem(col, self.nr))

    def has(self, i, j):
        row, col = self.row + i, self.col + j
        return (row >= 0) & (row < self.rows) & (col >= 0) & (col < self.cols)


class Halo:
    def __init__(self, tiling, image, rows, cols, bufs, raw=None):
        self.raw = raw
        self.tiling, self.image, self.rows, self.cols = tiling, image, rows, cols
        self.srow, self.scol, self.scor, self.rrow, self.rcol, self.rcor, self.ss, self.rs = bufs
        self.planes = image.shape[0]
        self.per = BLOCK // cols
        self.blocks = rows // self.per
        self.flat = image.reshape(self.planes, image.shape[1] * STRIDE, 128)

    def slot(self, i, j, bufs):
        row, col, cor = bufs
        if j == 0:
            return row.at[(i + 1) // 2]
        if i == 0:
            return col.at[(j + 1) // 2]
        return cor.at[(i + 1) + (j + 1) // 2]

    def copy(self, i, j):
        n = DIRS.index((i, j))
        if self.raw is not None and j == 0:
            source = self.raw[0].at[:, 0 if i == -1 else self.rows - 1]
        else:
            source = self.slot(i, j, (self.srow, self.scol, self.scor))
        return pltpu.make_async_remote_copy(
            src_ref=source,
            dst_ref=self.slot(i, j, (self.rrow, self.rcol, self.rcor)),
            send_sem=self.ss.at[n],
            recv_sem=self.rs.at[n],
            device_id=self.tiling.at(i, j),
            device_id_type=MESH,
        )

    def clear(self):
        for i, j in DIRS:
            if self.raw is not None and j == 0:
                continue

            @pl.when(jnp.logical_not(self.tiling.has(-i, -j)))
            def _():
                slot = self.slot(i, j, (self.rrow, self.rcol, self.rcor))
                slot[...] = jnp.zeros(slot.shape, slot.dtype)

    def start(self, dirs):
        for i, j in dirs:

            @pl.when(self.tiling.has(i, j))
            def _():
                self.copy(i, j).start()

    def send(self):
        cols, blocks = self.cols, self.blocks
        edge = {-1: (0, 8), 1: (blocks - 1, 8 + BLOCK - cols)}
        for p in range(self.planes):
            for i in (-1, 1):
                block, at = edge[i]
                if self.raw is None:
                    self.srow[(i + 1) // 2, p] = self.image[
                        p, block, at : at + cols, :
                    ].astype(BF16)
                for j in (-1, 1):
                    pixel = at + (cols - 1) * ((j + 1) // 2)
                    self.scor[(i + 1) + (j + 1) // 2, p] = jnp.broadcast_to(
                        self.image[p, block, pixel : pixel + 1, :], (16, 128)
                    ).astype(BF16)
            for j in (-1, 1):
                for inner in range(self.per):
                    start = 8 + inner * cols + (cols - 1) * ((j + 1) // 2)
                    self.scol[(j + 1) // 2, p, inner * blocks : (inner + 1) * blocks] = self.flat[
                        p, pl.ds(start, blocks, stride=STRIDE), :
                    ].astype(BF16)
        self.start([(i, j) for i, j in DIRS if self.raw is None or j != 0])

    def receive(self, targets, sides):
        cols, blocks = self.cols, self.blocks
        for i, j in DIRS:

            @pl.when(self.tiling.has(-i, -j))
            def _():
                self.copy(i, j).wait_recv()

        for n, target in enumerate(targets):
            for i in (-1, 1):
                if self.raw is not None:
                    here = self.tiling.has(-i, 0)

                    @pl.when(here)
                    def _():
                        place(self.image, 3 * n, blocks, self.raw[1](self.rrow[(i + 1) // 2, n], n))

                    @pl.when(jnp.logical_not(here))
                    def _():
                        place(self.image, 3 * n, blocks, jnp.zeros((BLOCK, C), F32))

                for t in range(3):
                    p = 3 * n + t
                    if self.raw is None:
                        self.image[p, blocks, 8 : 8 + cols, :] = self.rrow[
                            (i + 1) // 2, p
                        ].astype(F32)
                    for j, at in ((1, 7), (-1, 8 + cols)):
                        self.image[p, blocks, at : at + 1, :] = self.rcor[
                            (i + 1) + (j + 1) // 2, p
                        ].astype(F32)[0:1]
                row = 0 if i == 1 else self.rows + 1
                spread(self.image, 3 * n, blocks, cols, target.at[pl.ds(row, 1)])
            for j in (-1, 1):
                for t in range(3):
                    sides[(j + 1) // 2, t, 0 : self.rows // 8] = (
                        self.rcol[(j + 1) // 2, 3 * n + t]
                        .astype(F32)
                        .reshape(self.rows // 8, 8, 128)
                    )
            sub = lax.broadcasted_iota(jnp.int32, (16, 128), 0)
            lane = lax.broadcasted_iota(jnp.int32, (16, 128), 1)
            places = (
                (1, 0, 0, False),
                (1, 1, 128, False),
                (1, 2, 768, True),
                (0, 0, 512, False),
                (0, 1, 640, False),
                (0, 2, 896, True),
            )

            def fix(group, _):
                for s in range(8):
                    k = group * 8 + s
                    row = lax.rem(k, blocks) * self.per + k // blocks + 1
                    for side, t, lanes, leftover in places:
                        edge = (sub == 0) if side == 1 else (sub == 15)
                        if leftover:
                            edge = edge & (lane < 64)
                        at = 0 if side == 1 else cols - 16
                        pixel = jnp.broadcast_to(sides[side, t, group, s : s + 1, :], (16, 128))
                        held = target[row, at : at + 16, lanes : lanes + 128]
                        target[row, at : at + 16, lanes : lanes + 128] = jnp.where(
                            edge, pixel, held.astype(F32)
                        ).astype(BF16)
                return 0

            lax.fori_loop(0, self.rows // 8, fix, 0)

    def finish(self):
        for i, j in DIRS:

            @pl.when(self.tiling.has(i, j))
            def _():
                self.copy(i, j).wait_send()


def place(image, plane, block, value):
    image[plane, block, 8 : 8 + BLOCK, :] = value[:, 0:128]
    image[plane + 1, block, 8 : 8 + BLOCK, :] = value[:, 128:256]
    image[plane + 2, block, 8 : 8 + BLOCK, 0:64] = value[:, 256:320]


def spread(image, plane, block, cols, target):
    rows = target.shape[0]
    size = rows * cols
    rest = []
    for n, start in enumerate((7, 8, 9)):
        for t in range(2):
            piece = image[plane + t, block, start : start + size, :].astype(BF16)
            lanes = n * 256 + t * 128
            target[:, :, lanes : lanes + 128] = piece.reshape(rows, cols, 128)
        rest.append(image[plane + 2, block, start : start + size, :][:, 0:64])
    for lanes, pair in ((768, rest[0:2]), (896, [rest[2], jnp.zeros((size, 64), F32)])):
        piece = jnp.concatenate(pair, axis=1).astype(BF16)
        target[:, :, lanes : lanes + 128] = piece.reshape(rows, cols, 128)


def kernel(
    sizes,
    latent_hbm,
    control_hbm,
    first_hbm,
    branch_hbm,
    second_hbm,
    proj_hbm,
    first_mean,
    first_scale,
    first_gain,
    first_shift,
    first_bias,
    branch_mean,
    branch_scale,
    branch_gain,
    branch_shift,
    branch_bias,
    proj_bias,
    second_mean,
    second_scale,
    second_gain,
    second_shift,
    second_bias,
    outer,
    got,
    table,
    latent,
    control,
    all_w,
    rest_w,
    proj_w,
    cimage,
    bimage,
    cspread,
    bspread,
    hspread,
    crest,
    send,
    sides,
    *more,
):
    halo_bufs = [more[0:8], more[8:16], more[16:24]]
    load_sem, weight_sem, res_send, res_recv, own_sem = more[24:]
    g, c, r = (lax.axis_index(a) for a in ("group", "col", "row"))
    nr = sizes[2]
    ctile, btile = Tiling(sizes, "branch"), Tiling(sizes, "base")

    control_loads = [
        pltpu.make_async_copy(control_hbm.at[k], control.at[k], load_sem.at[k]) for k in range(2)
    ]
    for load in control_loads:
        load.start()

    barrier = pltpu.get_barrier_semaphore()
    count = nr - 1
    for tile in (ctile, btile):
        for i, j in DIRS:
            there = tile.has(i, j)
            count = count + there.astype(jnp.int32)

            @pl.when(there)
            def _():
                pl.semaphore_signal(
                    barrier, inc=1, device_id=tile.at(i, j), device_id_type=MESH
                )

    def peer(step):
        far = lax.rem(r // 2 + 1, 2) * 2
        core = lax.rem(r, 2)
        return (far + core, far + 1 - core, (r // 2) * 2 + 1 - core)[step]

    for step in range(3):
        pl.semaphore_signal(barrier, inc=1, device_id=(g, c, peer(step)), device_id_type=MESH)

    def act_control(value, branch):
        return swish(value.T.astype(F32), table, BRANCH + 2 * branch)

    chalo = Halo(ctile, cimage, CROWS, CCOLS, halo_bufs[0], raw=(control, act_control))
    bhalo = Halo(btile, bimage, BROWS, BCOLS, halo_bufs[1])
    hhalo = Halo(btile, bimage, BROWS, BCOLS, halo_bufs[2])

    norms = ((first_mean, first_scale, first_gain, first_shift, 0),) + tuple(
        (branch_mean, branch_scale, branch_gain, branch_shift, k) for k in range(2)
    ) + ((second_mean, second_scale, second_gain, second_shift, 0),)

    def vector(ref, k):
        return ref[...].reshape(1, -1) if len(ref.shape) == 1 else ref[k : k + 1, :]

    for n, (*stats, k) in enumerate(norms):
        mean, scale, gain, shift = (vector(ref, k) for ref in stats)
        slope = 0.5 * (widen(scale) * gain)
        table[2 * n : 2 * n + 1, :] = slope
        table[2 * n + 1 : 2 * n + 2, :] = 0.5 * shift - widen(mean) * slope
    table[BIAS : BIAS + 2, :] = branch_bias[...]
    table[BIAS + 2 : BIAS + 3, :] = proj_bias[0:1, :] + proj_bias[1:2, :]
    table[BIAS + 3 : BIAS + 4, :] = vector(first_bias, 0)
    table[BIAS + 4 : BIAS + 5, :] = vector(second_bias, 0)

    for load in control_loads:
        load.wait()
    latent_load = pltpu.make_async_copy(latent_hbm, latent, load_sem.at[2])
    proj_load = pltpu.make_async_copy(proj_hbm, proj_w, load_sem.at[3])

    def weight_loads(n):
        ref = (branch_hbm.at[0], branch_hbm.at[1], first_hbm, second_hbm)[n]
        return (pltpu.make_async_copy(ref, all_w.at[n], weight_sem.at[n]),)

    for load in (
        latent_load,
        *weight_loads(0),
        *weight_loads(1),
        proj_load,
        *weight_loads(2),
        *weight_loads(3),
    ):
        load.start()

    pl.semaphore_wait(barrier, count)
    chalo.start([(-1, 0), (1, 0)])
    for branch in range(2):

        def control_rows(n, _):
            for row in (4 * n, 4 * n + 1, 4 * n + 2, 4 * n + 3):
                value = act_control(control[branch, row], branch)
                place(cimage, 3 * branch, row, value)
                spread(cimage, 3 * branch, row, CCOLS, cspread.at[branch, pl.ds(row + 1, 1)])
            return 0

        lax.fori_loop(0, CROWS // 4, control_rows, 0)
    chalo.send()
    chalo.clear()
    bhalo.clear()
    hhalo.clear()

    def arrange(n):
        for load in weight_loads(n):
            load.wait()

        def tap_column(dx, _):
            for at, start, size in ((dx * 256, 0, 256), (768 + dx * 64, 256, 64)):
                pieces = [all_w[n, dy, dx, start : start + size, 256:320] for dy in range(3)]
                rest_w[n, pl.ds(at, size), :] = jnp.concatenate(
                    pieces + [jnp.zeros((size, 64), BF16)], axis=1
                )
            return 0

        lax.fori_loop(0, 3, tap_column, 0)
        rest_w[n, 960:1024, :] = jnp.zeros((64, 256), BF16)

    def main_dot(image_rows, n):
        weight = []
        for dy in range(3):
            weight += [all_w[n, dy, dx, 0:256, 0:256] for dx in range(3)]
            weight += [all_w[n, dy, dx, 256:320, 0:256] for dx in range(3)]
            weight.append(jnp.zeros((64, 256), BF16))
        return jnp.dot(
            jnp.concatenate(image_rows, axis=1),
            jnp.concatenate(weight, axis=0),
            preferred_element_type=F32,
        )

    def act_latent(n):
        value = swish(
            latent[pl.ds(n * 4, 4)].astype(F32).reshape(BLOCK, C), table, FIRST
        )
        place(bimage, 0, n, value)
        spread(bimage, 0, n, BCOLS, bspread.at[pl.ds(n * 4 + 1, 4)])

    def res_copy(step, part):
        q = peer(step)
        return pltpu.make_async_remote_copy(
            src_ref=send.at[q, part],
            dst_ref=got.at[r * 4 + part],
            send_sem=res_send.at[step, part],
            recv_sem=res_recv.at[step, part],
            device_id=(g, c, q),
            device_id_type=MESH,
        )

    def own_copy(part):
        return pltpu.make_async_copy(send.at[r, part], got.at[r * 4 + part], own_sem.at[part])

    def branch_part(part):
        row = part * PART
        first, last = (0, PART + 2) if part == 0 else (row + 2, row + PART + 2)
        features = []
        for branch in range(2):
            size = (last - first) * CCOLS
            crest[branch, first:last] = jnp.dot(
                cspread[branch, first:last].reshape(size, 1024),
                rest_w[branch],
                preferred_element_type=F32,
            ).reshape(last - first, CCOLS, 256)
            main = main_dot(
                [
                    cspread[branch, row + dy : row + dy + PART].reshape(PART * CCOLS, 1024)
                    for dy in range(3)
                ],
                branch,
            )
            rest = (
                crest[branch, row : row + PART, :, 0:64]
                + crest[branch, row + 1 : row + 1 + PART, :, 64:128]
                + crest[branch, row + 2 : row + 2 + PART, :, 128:192]
            ).reshape(PART * CCOLS, 64)
            bias = table[BIAS + branch : BIAS + branch + 1, :]
            features.append(
                ((main + bias[:, 0:256]).astype(BF16), (rest + bias[:, 256:320]).astype(BF16))
            )
        (m0, r0), (m1, r1) = features
        both = jnp.concatenate([m0, m1, jnp.concatenate([r0, r1], axis=1)], axis=1)
        proj = jnp.concatenate(
            [
                proj_w[0, 0:256, :],
                proj_w[1, 0:256, :],
                proj_w[0, 256:320, :],
                proj_w[1, 256:320, :],
            ],
            axis=0,
        )
        residual = jnp.dot(both, proj, preferred_element_type=F32) + table[BIAS + 2 : BIAS + 3, :]
        residual = residual.reshape(PART, CCOLS, C)
        for q in range(4):
            block = residual[:, q * BCOLS : (q + 1) * BCOLS, :].reshape(BLOCK, C)
            send[q, part, 0:128] = block[:, 0:128].astype(BF16)
            send[q, part, 128:256] = block[:, 128:256].astype(BF16)
            send[q, part, 256:320] = jnp.concatenate(
                [block[0:64, 256:320], block[64:128, 256:320]], axis=1
            ).astype(BF16)
        for step in range(3):
            res_copy(step, part).start()
        own_copy(part).start()

    def conv_base(n, image, row, bias_at):
        main = main_dot(
            [image[row + dy : row + dy + CHUNK].reshape(CHUNK * BCOLS, 1024) for dy in range(3)],
            n,
        )
        every = jnp.dot(
            image[row : row + CHUNK + 2].reshape((CHUNK + 2) * BCOLS, 1024),
            rest_w[n],
            preferred_element_type=F32,
        )
        size = CHUNK * BCOLS
        rest = (
            every[0:size, 0:64]
            + every[BCOLS : BCOLS + size, 64:128]
            + every[2 * BCOLS : 2 * BCOLS + size, 128:192]
        )
        bias = table[bias_at : bias_at + 1, :]
        return jnp.concatenate([main + bias[:, 0:256], rest + bias[:, 256:320]], axis=1)

    latent_load.wait()

    def latent_blocks(n, _):
        act_latent(2 * n)
        act_latent(2 * n + 1)
        return 0

    lax.fori_loop(0, BROWS // 8, latent_blocks, 0)
    bhalo.send()
    arrange(0)
    arrange(1)
    proj_load.wait()
    chalo.receive([cspread.at[0], cspread.at[1]], sides)
    branch_part(0)
    branch_part(1)
    arrange(2)

    bhalo.receive([bspread], sides)
    for row in range(0, BROWS, CHUNK):
        value = swish(conv_base(2, bspread, row, BIAS + 3), table, SECOND)
        for k in range(CHUNK // 4):
            place(bimage, 0, row // 4 + k, value[k * BLOCK : (k + 1) * BLOCK])
            spread(
                bimage, 0, row // 4 + k, BCOLS, hspread.at[pl.ds(row + 4 * k + 1, 4)]
            )
    hhalo.send()

    branch_part(2)
    branch_part(3)
    arrange(3)

    hhalo.receive([hspread], sides)
    for row in range(0, BROWS, CHUNK):
        value = conv_base(3, hspread, row, BIAS + 4).reshape(CHUNK, BCOLS, C)
        outer[row : row + CHUNK] = value + latent[row : row + CHUNK].astype(F32)

    for part in range(4):
        own_copy(part).wait()
        for step in range(3):
            res_copy(step, part).wait()
    for halo in (chalo, bhalo, hhalo):
        halo.finish()


def add_residual(outer, got, out_hbm, out, sem):
    def copy(n):
        rows = pl.ds(n * CHUNK, CHUNK)
        return pltpu.make_async_copy(out.at[rows], out_hbm.at[rows], sem.at[n])

    for n in range(BROWS // CHUNK):
        for k in range(n * CHUNK // 4, (n + 1) * CHUNK // 4):
            rows = slice(4 * k, 4 * k + 4)
            rest = got[k, 256:320]
            pieces = (
                got[k, 0:128],
                got[k, 128:256],
                jnp.concatenate([rest[:, 0:64], rest[:, 64:128]], axis=0),
            )
            for lanes, piece in zip((slice(0, 128), slice(128, 256), slice(256, 320)), pieces):
                total = outer[rows, :, lanes].reshape(BLOCK, -1) + piece.astype(F32)
                out[rows, :, lanes] = total.astype(BF16).reshape(4, BCOLS, -1)
        copy(n).start()
    for n in range(BROWS // CHUNK):
        copy(n).wait()


def halo_scratch(planes, rows, cols, raw=False):
    row = pltpu.VMEM((2, 2, C, 128) if raw else (2, planes, cols, 128), BF16)
    both = [
        row,
        pltpu.VMEM((2, planes, rows, 128), BF16),
        pltpu.VMEM((4, planes, 16, 128), BF16),
    ]
    send = [pltpu.VMEM((8, 128), BF16)] + both[1:] if raw else both
    return send + both + [pltpu.SemaphoreType.DMA((8,)), pltpu.SemaphoreType.DMA((8,))]


def body(
    sizes,
    latent,
    control,
    first_mean,
    first_scale,
    first_gain,
    first_shift,
    first_kernel,
    first_bias,
    branch_mean,
    branch_scale,
    branch_gain,
    branch_shift,
    branch_kernel,
    branch_bias,
    proj_weight,
    proj_bias,
    second_mean,
    second_scale,
    second_gain,
    second_shift,
    second_kernel,
    second_bias,
):
    hbm = pl.BlockSpec(memory_space=pl.ANY)
    vmem = pl.BlockSpec(memory_space=pltpu.VMEM)
    outer, residual = pl.pallas_call(
        functools.partial(kernel, sizes),
        out_shape=(
            pltpu.VMEM((BROWS, BCOLS, C), F32),
            pltpu.VMEM((16, 320, 128), BF16),
        ),
        in_specs=[hbm] * 6 + [vmem] * 16,
        out_specs=(vmem, vmem),
        scratch_shapes=[
            pltpu.VMEM((16, C), F32),
            pltpu.VMEM((BROWS, BCOLS, C), BF16),
            pltpu.VMEM((2, CROWS, C, CCOLS), BF16),
            pltpu.VMEM((4, 3, 3, C, C), BF16),
            pltpu.VMEM((4, 1024, 256), BF16),
            pltpu.VMEM((2, C, C), BF16),
            pltpu.VMEM((6, CROWS + 1, STRIDE, 128), F32),
            pltpu.VMEM((3, BROWS // 4 + 1, STRIDE, 128), F32),
            pltpu.VMEM((2, CROWS + 2, CCOLS, 1024), BF16),
            pltpu.VMEM((BROWS + 2, BCOLS, 1024), BF16),
            pltpu.VMEM((BROWS + 2, BCOLS, 1024), BF16),
            pltpu.VMEM((2, CROWS + 2, CCOLS, 256), F32),
            pltpu.VMEM((4, 4, 320, 128), BF16),
            pltpu.VMEM((2, 3, BROWS // 8, 8, 128), F32),
        ]
        + halo_scratch(6, CROWS, CCOLS, raw=True)
        + halo_scratch(3, BROWS, BCOLS)
        + halo_scratch(3, BROWS, BCOLS)
        + [
            pltpu.SemaphoreType.DMA((4,)),
            pltpu.SemaphoreType.DMA((4,)),
            pltpu.SemaphoreType.DMA((3, 4)),
            pltpu.SemaphoreType.DMA((3, 4)),
            pltpu.SemaphoreType.DMA((4,)),
        ],
        compiler_params=pltpu.CompilerParams(
            collective_id=0, has_side_effects=True, vmem_limit_bytes=VMEM_LIMIT
        ),
    )(
        latent,
        jnp.transpose(control, (0, 1, 3, 2)),
        first_kernel,
        branch_kernel,
        second_kernel,
        proj_weight,
        first_mean,
        first_scale,
        first_gain,
        first_shift,
        first_bias,
        branch_mean,
        branch_scale,
        branch_gain,
        branch_shift,
        branch_bias,
        proj_bias,
        second_mean,
        second_scale,
        second_gain,
        second_shift,
        second_bias,
    )
    return pl.pallas_call(
        add_residual,
        out_shape=jax.ShapeDtypeStruct((BROWS, BCOLS, C), BF16),
        in_specs=[vmem, vmem],
        out_specs=hbm,
        scratch_shapes=[
            pltpu.VMEM((BROWS, BCOLS, C), BF16),
            pltpu.SemaphoreType.DMA((BROWS // CHUNK,)),
        ],
        compiler_params=pltpu.CompilerParams(vmem_limit_bytes=16 * 2**20),
    )(outer, residual)


def solution(mesh):
    sizes = (mesh.shape["group"], mesh.shape["col"], mesh.shape["row"])
    in_specs = (
        P("group", ("col", "row"), None),
        P(None, ("group", "row"), "col", None),
    ) + (P(),) * 20
    out_specs = P("group", ("col", "row"), None)
    return jax.shard_map(
        functools.partial(body, sizes),
        mesh=mesh,
        in_specs=in_specs,
        out_specs=out_specs,
        check_vma=False,
    )
```
